512 devices in a mesh: tm: 32 (over y, z_lo), row: 16 (over x, z_hi, core).
Axes of the slice: x: 4, y: 8, z: 8 (z_hi: 2, z_lo: 4; z = z_hi * 4 + z_lo), core: 2. Of those that a mesh axis runs over, the one named last changes fastest.
Arguments:
- latents: bfloat16 [64, 96, 80, 256], P('tm', 'row'), may hold values from -6 to 6
- conv_weight: bfloat16 [3, 3, 768, 256], replicated, may hold values from -0.078125 to 0.078125
- norm_gain: float32 [256], replicated, may hold values from 0.1 to 1.9
- depth_target: bfloat16 [64, 96, 80, 128], P('tm', 'row'), may hold values from -6 to 6
Outputs:
- features: bfloat16 [64, 96, 80, 256], P('tm', 'row')
- gram: float32 [256, 256], replicated
- cross: float32 [256, 128], replicated
The draws below stay inside these ranges and needn't reach their ends.
All inputs are finite; a program needn't handle non-finite values.
Results may differ from the reference program's by a relative error of at most 0.003.
Values may be sent and summed in bfloat16 or wider, within the bound.
A program may use at most 64 MiB of HBM per device.

```python
import jax
import jax.numpy as jnp
from jax import lax

C = 256
BINS = 128
COLS = 80
FRAMES = 64
ROWS = 96


def levels(stream_key, dims, cuts, least, largest):
    def one(position, parts):
        draws = jax.random.uniform(jax.random.fold_in(jax.random.fold_in(stream_key, 6), position), (parts,), jnp.float32, least / len(cuts), largest / len(cuts))
        return jnp.repeat(jnp.exp(draws), dims[position] // parts).reshape((-1,) + (1,) * (len(dims) - position - 1))

    loudness = one(*cuts[0])
    for cut in cuts[1:]:
        loudness = loudness * one(*cut)
    return loudness


def centred(key, extent, deviation, most, cuts=(), kind=jnp.bfloat16):
    array = deviation * jax.random.normal(key, extent, jnp.float32)
    if cuts:
        array = array * levels(key, extent, cuts, -0.22, 0.18)
    return jnp.clip(array, -most, most).astype(kind)


def setup_inputs(seed: int = 0) -> dict:
    splits = jax.random.split(jax.random.key(seed), 5)
    latents = centred(splits[0], (FRAMES, ROWS, COLS, C), 1.0, 6.0, ((0, 32), (1, 16)))
    conv_weight = centred(splits[1], (3, 3, 3 * C, C), (27 * C) ** -0.5, 0.078125)
    norm_gain = jnp.clip(1.0 + 0.18 * jax.random.normal(splits[2], (C,), jnp.float32), 0.1, 1.9)
    depth_target = centred(splits[3], (FRAMES, ROWS, COLS, BINS), 1.0, 6.0, ((0, 32), (1, 16)))
    return {"latents": latents, "conv_weight": conv_weight, "norm_gain": norm_gain, "depth_target": depth_target}


def convolve(padded, conv_weight):
    frames = padded.shape[0] - 2
    rows = padded.shape[1] - 2
    cols = padded.shape[2]
    chans = conv_weight.shape[3]
    wide = jnp.pad(padded, ((0, 0), (0, 0), (1, 1), (0, 0)))
    stacked = jnp.concatenate([wide[:, :, 0:cols], wide[:, :, 1:cols + 1], wide[:, :, 2:cols + 2]], axis=3)
    total = jnp.zeros((frames * rows * cols, chans), jnp.float32)
    for dtime in range(3):
        for drow in range(3):
            piece = stacked[dtime:dtime + frames, drow:drow + rows].reshape(frames * rows * cols, -1)
            total = total + jnp.dot(piece, conv_weight[dtime, drow], preferred_element_type=jnp.float32)
    return total

def make_features(latents, conv, norm_gain):
    flat = latents.reshape(conv.shape[0], conv.shape[1]).astype(jnp.float32)
    normed = conv * jax.lax.rsqrt(lax.optimization_barrier(jnp.mean(conv * conv, axis=1, keepdims=True)) + 1e-06) * norm_gain
    return (flat + jax.nn.silu(normed)).astype(jnp.bfloat16)

def reference(latents, conv_weight, norm_gain, depth_target):
    padded = jnp.pad(latents, ((2, 0), (1, 1), (0, 0), (0, 0)))
    conv = convolve(padded, conv_weight)
    flat = make_features(latents, conv, norm_gain)
    targets = depth_target.reshape(flat.shape[0], -1)
    count = flat.shape[0]
    gram = jnp.dot(flat.T, flat, preferred_element_type=jnp.float32) / count
    cross = jnp.dot(flat.T, targets, preferred_element_type=jnp.float32) / count
    return (flat.reshape(latents.shape), gram, cross)
```

```python
import functools

import jax
import jax.numpy as jnp
from jax import lax
from jax.experimental import pallas as pl
from jax.experimental.pallas import tpu as pltpu
from jax.sharding import PartitionSpec as P

MESH = pl.DeviceIdType.MESH
FAR = (4, 3, 5, 2, 6, 1, 7)


def reduce_kernel(scale, g_ref, c_ref, gram_ref, cross_ref, pay, rs, ya, za, yb, zb, fin, send_sem, recv_sem):
    tm = lax.axis_index("tm")
    row = lax.axis_index("row")
    y, zl = tm // 4, tm % 4
    x, zh, core = row // 4, (row // 2) % 2, row % 2

    def a_peer(j):
        return tm, (j // 2) * 4 + zh * 2 + j % 2

    def y_peer(j):
        return j * 4 + zl, row

    def z_peer(j):
        return y * 4 + j % 4, x * 4 + (j // 4) * 2 + core

    a_me, y_me, z_me = x * 2 + core, y, zh * 4 + zl
    groups = ((a_me, a_peer), (y_me, y_peer), (z_me, z_peer))

    barrier = pltpu.get_barrier_semaphore()
    for me, peer in groups:
        for k in range(1, 8):
            pl.semaphore_signal(barrier, inc=1, device_id=peer((me + k) % 8), device_id_type=MESH)
    pay[0:128] = g_ref[0:128, 0:128]
    pay[128:256] = g_ref[0:128, 128:256]
    pay[256:384] = g_ref[128:256, 128:256]
    pay[384:640] = c_ref[...]
    pl.semaphore_wait(barrier, 21)

    def copy(stage, me, peer, k, src, dst):
        j = (me + k) % 8
        return pltpu.make_async_remote_copy(
            src_ref=src(j), dst_ref=dst(me), send_sem=send_sem.at[stage, j], recv_sem=recv_sem.at[stage, me],
            device_id=peer(j), device_id_type=MESH,
        )

    def arrival(stage, me, peer, k, src, dst):
        j = (me + k) % 8
        return pltpu.make_async_remote_copy(
            src_ref=src(j), dst_ref=dst(j), send_sem=send_sem.at[stage, j], recv_sem=recv_sem.at[stage, j],
            device_id=peer(j), device_id_type=MESH,
        )

    def send(stage, me, peer, src, dst):
        for k in FAR:
            copy(stage, me, peer, k, src, dst).start()

    def receive(stage, me, peer, src, dst):
        for k in FAR:
            arrival(stage, me, peer, k, src, dst).wait_recv()

    def drain(stage, me, peer, src, dst):
        for k in FAR:
            copy(stage, me, peer, k, src, dst).wait_send()

    def chunk(ref):
        return lambda j: ref.at[pl.ds(pl.multiple_of(j * 80, 8), 80)]

    def slot(ref):
        return lambda j: ref.at[j]

    def total(ref):
        acc = ref[0]
        for j in range(1, 8):
            acc = acc + ref[j]
        return acc

    s0 = (0, a_me, a_peer, chunk(pay), slot(rs))
    send(*s0)
    rs[a_me] = pay[pl.ds(pl.multiple_of(a_me * 80, 8), 80)]
    receive(*s0)
    part = total(rs)
    ya[y_me] = part[0:40]
    za[z_me] = part[40:80]
    s1 = (1, y_me, y_peer, lambda j: ya.at[y_me], slot(ya))
    s2 = (2, z_me, z_peer, lambda j: za.at[z_me], slot(za))
    send(*s1)
    send(*s2)
    receive(*s1)
    zb[z_me] = total(ya)
    s3 = (3, z_me, z_peer, lambda j: zb.at[z_me], slot(zb))
    send(*s3)
    receive(*s2)
    yb[y_me] = total(za)
    s4 = (4, y_me, y_peer, lambda j: yb.at[y_me], slot(yb))
    send(*s4)
    receive(*s3)
    here = pl.multiple_of(a_me * 80, 8)
    fin[pl.ds(here, 40)] = total(zb)
    receive(*s4)
    fin[pl.ds(here + 40, 40)] = total(yb)
    s5 = (5, a_me, a_peer, lambda j: fin.at[pl.ds(here, 80)], chunk(fin))
    send(*s5)
    receive(*s5)
    gram_ref[0:128, 0:128] = fin[0:128] * scale
    gram_ref[0:128, 128:256] = fin[128:256] * scale
    gram_ref[128:256, 0:128] = fin[128:256].T * scale
    gram_ref[128:256, 128:256] = fin[256:384] * scale
    cross_ref[...] = fin[384:640] * scale
    for s in (s0, s1, s2, s3, s4, s5):
        drain(*s)


def reduce_all(gram, cross, count):
    vmem = pl.BlockSpec(memory_space=pltpu.VMEM)
    f32 = jnp.float32
    return pl.pallas_call(
        functools.partial(reduce_kernel, 1.0 / count),
        out_shape=(jax.ShapeDtypeStruct((256, 256), f32), jax.ShapeDtypeStruct((256, 128), f32)),
        in_specs=[vmem, vmem],
        out_specs=(vmem, vmem),
        scratch_shapes=[
            pltpu.VMEM((640, 128), f32),
            pltpu.VMEM((8, 80, 128), f32),
            pltpu.VMEM((8, 40, 128), f32),
            pltpu.VMEM((8, 40, 128), f32),
            pltpu.VMEM((8, 40, 128), f32),
            pltpu.VMEM((8, 40, 128), f32),
            pltpu.VMEM((640, 128), f32),
            pltpu.SemaphoreType.DMA((6, 8)),
            pltpu.SemaphoreType.DMA((6, 8)),
        ],
        compiler_params=pltpu.CompilerParams(collective_id=0, has_side_effects=True),
    )(gram, cross)


def from_behind(value, axis, steps):
    count = lax.axis_size(axis)
    first, last = (max(0, -steps), min(count, count - steps))
    return lax.ppermute(value, axis, [(source, source + steps) for source in range(first, last)])


def extended(cells, sides, width):
    for axis, dim in sides:
        count = lax.axis_size(axis)
        ends = count - 1
        head = lax.slice_in_dim(cells, 0, width, axis=dim)
        tail = lax.slice_in_dim(cells, cells.shape[dim] - width, cells.shape[dim], axis=dim)
        cells = jnp.concatenate(
            [
                lax.ppermute(tail, axis, [(i, (i + 1) % count) for i in range(ends)]),
                cells,
                lax.ppermute(head, axis, [((i + 1) % count, i) for i in range(ends)]),
            ],
            axis=dim,
        )
    return cells


def convolve(padded, conv_weight):
    frames = padded.shape[0] - 2
    rows = padded.shape[1] - 2
    cols = padded.shape[2]
    chans = conv_weight.shape[3]
    wide = jnp.pad(padded, ((0, 0), (0, 0), (1, 1), (0, 0)))
    stacked = jnp.concatenate(
        [wide[:, :, 0:cols], wide[:, :, 1 : cols + 1], wide[:, :, 2 : cols + 2]], axis=3
    )
    total = jnp.zeros((frames * rows * cols, chans), jnp.float32)
    for dtime in range(3):
        for drow in range(3):
            piece = stacked[dtime : dtime + frames, drow : drow + rows].reshape(
                frames * rows * cols, -1
            )
            total = total + jnp.dot(
                piece, conv_weight[dtime, drow], preferred_element_type=jnp.float32
            )
    return total


def on_device(latents, conv_weight, norm_gain, depth_target):
    cached = from_behind(latents, "tm", 1)
    joined = jnp.concatenate([cached, latents], axis=0)
    padded = extended(joined, (("row", 1),), 1)
    conv = convolve(padded, conv_weight)
    flat_in = latents.reshape(conv.shape[0], conv.shape[1]).astype(jnp.float32)
    normed = conv * jax.lax.rsqrt(jnp.mean(conv * conv, axis=1, keepdims=True) + 1e-06) * norm_gain
    flat = (flat_in + jax.nn.silu(normed)).astype(jnp.bfloat16)
    targets = depth_target.reshape(flat.shape[0], -1)
    gram_part = jnp.dot(flat.T, flat, preferred_element_type=jnp.float32)
    cross_part = jnp.dot(flat.T, targets, preferred_element_type=jnp.float32)
    count = flat.shape[0] * lax.axis_size("tm") * lax.axis_size("row")
    gram, cross = reduce_all(gram_part, cross_part, count)
    return (flat.reshape(latents.shape), gram, cross)


def solution(mesh):
    in_specs = (P("tm", "row", None, None), P(), P(), P("tm", "row", None, None))
    out_specs = (P("tm", "row", None, None), P(), P())
    return jax.shard_map(
        on_device, mesh=mesh, in_specs=in_specs, out_specs=out_specs, check_vma=False
    )
```

```python
import functools

import jax
import jax.numpy as jnp
from jax import lax
from jax.experimental import pallas as pl
from jax.experimental.pallas import tpu as pltpu
from jax.sharding import PartitionSpec as P

MESH = pl.DeviceIdType.MESH
FAR = (4, 3, 5, 2, 6, 1, 7)
F32, BF16 = jnp.float32, jnp.bfloat16
OWN = (((0, 2),), ((0, 1), (1, 2)))
NEXT = (((0, 0), (1, 1)), ((1, 0),))


def layer_kernel(
    lat_hbm, w_hbm, gain_ref, tgt_hbm, feat, fin,
    win, w, tgt, own, nxt, halo, conv_in, conv_edge, zin_out, zin, zed_out, zed,
    pay, rs, ya, za, yb, zb, load_sem, side_send, side_recv, z_send, z_recv, send_sem, recv_sem,
):
    tm = lax.axis_index("tm")
    row = lax.axis_index("row")
    y, zl = tm // 4, tm % 4
    x, zh, core = row // 4, (row // 2) % 2, row % 2

    def a_peer(j):
        return tm, (j // 2) * 4 + zh * 2 + j % 2

    def y_peer(j):
        return j * 4 + zl, row

    def z_peer(j):
        return y * 4 + j % 4, x * 4 + (j // 4) * 2 + core

    a_me, y_me, z_me = x * 2 + core, y, zh * 4 + zl
    has_prev, has_next, has_up, has_down = tm > 0, tm < 31, row > 0, row < 15

    barrier = pltpu.get_barrier_semaphore()
    near = ((has_prev, (tm - 1, row)), (has_next, (tm + 1, row)), (has_up, (tm, row - 1)), (has_down, (tm, row + 1)))
    expected = jnp.int32(21)
    for there, device in near:
        @pl.when(there)
        def _():
            pl.semaphore_signal(barrier, inc=1, device_id=device, device_id_type=MESH)
        expected = expected + there.astype(jnp.int32)
    for me, peer in ((a_me, a_peer), (y_me, y_peer), (z_me, z_peer)):
        for k in range(1, 8):
            pl.semaphore_signal(barrier, inc=1, device_id=peer((me + k) % 8), device_id_type=MESH)

    loads = [pltpu.make_async_copy(lat_hbm, win.at[:, 1:7], load_sem.at[0])]
    loads += [pltpu.make_async_copy(w_hbm.at[dt], w.at[dt], load_sem.at[1 + dt]) for dt in range(3)]
    loads += [pltpu.make_async_copy(tgt_hbm, tgt, load_sem.at[4])]
    for load in loads:
        load.start()
    blank = jnp.zeros((2, 80, 256), BF16)
    win[:, 0] = blank
    win[:, 7] = blank

    @pl.when(row == 0)
    def _():
        halo[0] = blank

    @pl.when(row == 15)
    def _():
        halo[1] = blank

    @pl.when(tm == 0)
    def _():
        zin[...] = jnp.zeros(zin.shape, BF16)
        zed[...] = jnp.zeros(zed.shape, BF16)

    def taps(dst, outs):
        @pl.loop(0, 3)
        def _(dw):
            cols = pl.ds(pl.multiple_of(dw * 256, 256), 256)
            for o, pairs in enumerate(outs):
                acc = None
                for frame, dt in pairs:
                    for dh in range(3):
                        piece = win[frame, dh : dh + 6].reshape(480, 256)
                        prod = jnp.dot(piece, w[dt, dh, cols], preferred_element_type=F32)
                        acc = prod if acc is None else acc + prod
                dst[o, dw] = acc

    def joined(src, o, rows, size):
        col = lax.broadcasted_iota(jnp.int32, (size, 1), 0) % 80
        left = jnp.where(col == 0, 0.0, pltpu.roll(src[o, 0, rows], 1, 0))
        right = jnp.where(col == 79, 0.0, pltpu.roll(src[o, 2, rows], size - 1, 0))
        return src[o, 1, rows] + left + right

    for load in loads[:3]:
        load.wait()
    taps(nxt, NEXT)
    for f in range(2):
        zin_out[f] = joined(nxt, f, pl.ds(80, 320), 320).astype(BF16).reshape(4, 80, 256)
    pl.semaphore_wait(barrier, expected)

    def side_copy(to):
        return pltpu.make_async_remote_copy(
            src_ref=win.at[:, 6 - 5 * to], dst_ref=halo.at[to], send_sem=side_send.at[to], recv_sem=side_recv.at[to],
            device_id=(tm, row + 1 - 2 * to), device_id_type=MESH,
        )

    def inner_copy(f):
        return pltpu.make_async_remote_copy(
            src_ref=zin_out.at[f], dst_ref=zin.at[f], send_sem=z_send.at[f], recv_sem=z_recv.at[f],
            device_id=(tm + 1, row), device_id_type=MESH,
        )

    def edge_copy(side):
        return pltpu.make_async_remote_copy(
            src_ref=zed_out.at[side], dst_ref=zed.at[side], send_sem=z_send.at[2 + side], recv_sem=z_recv.at[2 + side],
            device_id=(tm + 1, row), device_id_type=MESH,
        )

    @pl.when(has_down)
    def _():
        side_copy(0).start()

    @pl.when(has_up)
    def _():
        side_copy(1).start()

    @pl.when(has_next)
    def _():
        inner_copy(0).start()
        inner_copy(1).start()

    loads[3].wait()
    taps(own, OWN)
    for f in range(2):
        conv_in[f] = joined(own, f, pl.ds(80, 320), 320)

    def side_step(i, carry):
        side = (1 - core) * (1 - i) + core * i
        other = row + 2 * side - 1

        @pl.when((other >= 0) & (other <= 15))
        def _():
            side_copy(side).wait_recv()

        dh = 2 * side
        rows = pl.ds(pl.multiple_of(side * 400, 80), 80)

        @pl.loop(0, 3)
        def _(dw):
            cols = pl.ds(pl.multiple_of(dw * 256, 256), 256)
            both = halo[side].reshape(160, 256)
            p0 = jnp.dot(both, w[0, dh, cols], preferred_element_type=F32)
            p1 = jnp.dot(both[80:160], w[1, dh, cols], preferred_element_type=F32)
            nxt[0, dw, rows] += p0[0:80] + p1
            nxt[1, dw, rows] += p0[80:160]

        for f in range(2):
            zed_out[side, f] = joined(nxt, f, rows, 80).astype(BF16)

        @pl.when(has_next)
        def _():
            edge_copy(side).start()

        @pl.loop(0, 3)
        def _(dw):
            cols = pl.ds(pl.multiple_of(dw * 256, 256), 256)
            both = halo[side].reshape(160, 256)
            p0 = jnp.dot(both, w[2, dh, cols], preferred_element_type=F32)
            p1 = jnp.dot(both[0:80], w[1, dh, cols], preferred_element_type=F32)
            own[0, dw, rows] += p0[0:80]
            own[1, dw, rows] += p0[80:160] + p1

        for f in range(2):
            conv_edge[side, f] = joined(own, f, rows, 80)
        return carry

    lax.fori_loop(0, 2, side_step, 0)
    loads[4].wait()

    def finish(conv, base, target, first):
        size = conv.shape[0]
        mean = jnp.mean(conv * conv, axis=1, keepdims=True)
        v = conv * lax.rsqrt(mean + 1e-06) * gain_ref[...][None, :]
        out = (base.reshape(size, 256).astype(F32) + v / (1.0 + jnp.exp(-v))).astype(BF16)
        dims = (((0,), (0,)), ((), ()))
        g = lax.dot_general(out, out, dims, preferred_element_type=F32)
        c = lax.dot_general(out, target.reshape(size, 128), dims, preferred_element_type=F32)
        for i, block in enumerate((g[0:128, 0:128], g[0:128, 128:256], g[128:256, 128:256], c[0:128], c[128:256])):
            place = slice(128 * i, 128 * i + 128)
            pay[place] = block if first else pay[place] + block
        return out

    for f in range(2):
        @pl.when(has_prev)
        def _():
            inner_copy(f).wait_recv()

        conv = conv_in[f] + zin[f].reshape(320, 256).astype(F32)
        feat[f, 1:5] = finish(conv, win[f, 2:6], tgt[f, 1:5], f == 0).reshape(4, 80, 256)
    for side in range(2):
        @pl.when(has_prev)
        def _():
            edge_copy(side).wait_recv()

    conv = (conv_edge[...] + zed[...].astype(F32)).reshape(320, 256)
    base = jnp.concatenate([win[:, 1], win[:, 6]], axis=0)
    target = jnp.concatenate([tgt[:, 0], tgt[:, 5]], axis=0)
    out = finish(conv, base, target, False).reshape(2, 2, 80, 256)
    feat[:, 0] = out[0]
    feat[:, 5] = out[1]

    def copy(stage, me, peer, k, src, dst):
        j = (me + k) % 8
        return pltpu.make_async_remote_copy(
            src_ref=src(j), dst_ref=dst(me), send_sem=send_sem.at[stage, j], recv_sem=recv_sem.at[stage, me],
            device_id=peer(j), device_id_type=MESH,
        )

    def arrival(stage, me, peer, k, src, dst):
        j = (me + k) % 8
        return pltpu.make_async_remote_copy(
            src_ref=src(j), dst_ref=dst(j), send_sem=send_sem.at[stage, j], recv_sem=recv_sem.at[stage, j],
            device_id=peer(j), device_id_type=MESH,
        )

    def send(stage, me, peer, src, dst):
        for k in FAR:
            copy(stage, me, peer, k, src, dst).start()

    def receive(stage, me, peer, src, dst):
        for k in FAR:
            arrival(stage, me, peer, k, src, dst).wait_recv()

    def drain(stage, me, peer, src, dst):
        for k in FAR:
            copy(stage, me, peer, k, src, dst).wait_send()

    def chunk(ref):
        return lambda j: ref.at[pl.ds(pl.multiple_of(j * 80, 8), 80)]

    def slot(ref):
        return lambda j: ref.at[j]

    def total(ref):
        acc = ref[0].astype(F32)
        for j in range(1, 8):
            acc = acc + ref[j].astype(F32)
        return acc

    s0 = (0, a_me, a_peer, chunk(pay), slot(rs))
    send(*s0)
    rs[a_me] = pay[pl.ds(pl.multiple_of(a_me * 80, 8), 80)]
    receive(*s0)
    part = total(rs)
    ya[y_me] = part[0:48].astype(BF16)
    za[z_me] = part[48:80].astype(BF16)
    s1 = (1, y_me, y_peer, lambda j: ya.at[y_me], slot(ya))
    s2 = (2, z_me, z_peer, lambda j: za.at[z_me], slot(za))
    send(*s1)
    send(*s2)
    receive(*s1)
    zb[z_me] = total(ya).astype(BF16)
    s3 = (3, z_me, z_peer, lambda j: zb.at[z_me], slot(zb))
    send(*s3)
    receive(*s2)
    yb[y_me] = total(za).astype(BF16)
    s4 = (4, y_me, y_peer, lambda j: yb.at[y_me], slot(yb))
    send(*s4)
    receive(*s3)
    here = pl.multiple_of(a_me * 80, 8)
    fin[pl.ds(here, 48)] = total(zb)
    receive(*s4)
    fin[pl.ds(here + 48, 32)] = total(yb)
    s5 = (5, a_me, a_peer, lambda j: fin.at[pl.ds(here, 80)], chunk(fin))
    send(*s5)
    receive(*s5)

    for s in (s0, s1, s2, s3, s4, s5):
        drain(*s)

    @pl.when(has_down)
    def _():
        side_copy(0).wait_send()

    @pl.when(has_up)
    def _():
        side_copy(1).wait_send()

    @pl.when(has_next)
    def _():
        for i in range(2):
            inner_copy(i).wait_send()
            edge_copy(i).wait_send()


def write_kernel(scale, feat, fin, feat_out, gram_out, cross_out, gram, cross, sem):
    first = pltpu.make_async_copy(feat, feat_out, sem.at[0])
    first.start()
    cross[...] = fin[384:640] * scale
    second = pltpu.make_async_copy(cross, cross_out, sem.at[1])
    second.start()
    gram[0:128, 0:128] = fin[0:128] * scale
    gram[0:128, 128:256] = fin[128:256] * scale
    gram[128:256, 0:128] = fin[128:256].T * scale
    gram[128:256, 128:256] = fin[256:384] * scale
    third = pltpu.make_async_copy(gram, gram_out, sem.at[2])
    third.start()
    first.wait()
    second.wait()
    third.wait()


def on_device(latents, conv_weight, norm_gain, depth_target):
    vmem = pl.BlockSpec(memory_space=pltpu.VMEM)
    anywhere = pl.BlockSpec(memory_space=pltpu.HBM)
    dma = pltpu.SemaphoreType.DMA
    feat, fin = pl.pallas_call(
        layer_kernel,
        out_shape=(jax.ShapeDtypeStruct((2, 6, 80, 256), BF16), jax.ShapeDtypeStruct((640, 128), F32)),
        in_specs=[anywhere, anywhere, vmem, anywhere],
        out_specs=(vmem, vmem),
        scratch_shapes=[
            pltpu.VMEM((2, 8, 80, 256), BF16),
            pltpu.VMEM((3, 3, 768, 256), BF16),
            pltpu.VMEM((2, 6, 80, 128), BF16),
            pltpu.VMEM((2, 3, 480, 256), F32),
            pltpu.VMEM((2, 3, 480, 256), F32),
            pltpu.VMEM((2, 2, 80, 256), BF16),
            pltpu.VMEM((2, 320, 256), F32),
            pltpu.VMEM((2, 2, 80, 256), F32),
            pltpu.VMEM((2, 4, 80, 256), BF16),
            pltpu.VMEM((2, 4, 80, 256), BF16),
            pltpu.VMEM((2, 2, 80, 256), BF16),
            pltpu.VMEM((2, 2, 80, 256), BF16),
            pltpu.VMEM((640, 128), F32),
            pltpu.VMEM((8, 80, 128), F32),
            pltpu.VMEM((8, 48, 128), BF16),
            pltpu.VMEM((8, 32, 128), BF16),
            pltpu.VMEM((8, 32, 128), BF16),
            pltpu.VMEM((8, 48, 128), BF16),
            dma((5,)),
            dma((2,)),
            dma((2,)),
            dma((4,)),
            dma((4,)),
            dma((6, 8)),
            dma((6, 8)),
        ],
        compiler_params=pltpu.CompilerParams(collective_id=0, has_side_effects=True, vmem_limit_bytes=55_200_000),
    )(latents, conv_weight, norm_gain, depth_target)
    count = 960 * lax.axis_size("tm") * lax.axis_size("row")
    return pl.pallas_call(
        functools.partial(write_kernel, 1.0 / count),
        out_shape=(
            jax.ShapeDtypeStruct((2, 6, 80, 256), BF16),
            jax.ShapeDtypeStruct((256, 256), F32),
            jax.ShapeDtypeStruct((256, 128), F32),
        ),
        in_specs=[vmem, vmem],
        out_specs=(anywhere, anywhere, anywhere),
        scratch_shapes=[pltpu.VMEM((256, 256), F32), pltpu.VMEM((256, 128), F32), dma((3,))],
        compiler_params=pltpu.CompilerParams(vmem_limit_bytes=55_200_000),
    )(feat, fin)


def solution(mesh):
    in_specs = (P("tm", "row", None, None), P(), P(), P("tm", "row", None, None))
    out_specs = (P("tm", "row", None, None), P(), P())
    return jax.shard_map(
        on_device, mesh=mesh, in_specs=in_specs, out_specs=out_specs, check_vma=False
    )
```

```python
import functools

import jax
import jax.numpy as jnp
from jax import lax
from jax.experimental import pallas as pl
from jax.experimental.pallas import tpu as pltpu
from jax.sharding import PartitionSpec as P

MESH = pl.DeviceIdType.MESH
FAR = (4, 3, 5, 2, 6, 1, 7)
F32, BF16 = jnp.float32, jnp.bfloat16
OWN = (((0, 2),), ((0, 1), (1, 2)))
NEXT = (((0, 0), (1, 1)), ((1, 0),))


def layer_kernel(
    lat_hbm, w_hbm, gain_hbm, tgt_hbm, feat, fin,
    win, w, tgt, gain_ref, own, nxt, halo, conv_in, conv_edge, zin_out, zin, zed_out, zed,
    sums, gpay, grs, crs, ya, za, yb, zb, load_sem, side_send, side_recv, z_send, z_recv, send_sem, recv_sem,
):
    tm = lax.axis_index("tm")
    row = lax.axis_index("row")
    y, zl = tm // 4, tm % 4
    x, zh, core = row // 4, (row // 2) % 2, row % 2

    def a_peer(j):
        return tm, (j // 2) * 4 + zh * 2 + j % 2

    def y_peer(j):
        return j * 4 + zl, row

    def z_peer(j):
        return y * 4 + j % 4, x * 4 + (j // 4) * 2 + core

    a_me, y_me, z_me = x * 2 + core, y, zh * 4 + zl
    has_prev, has_next, has_up, has_down = tm > 0, tm < 31, row > 0, row < 15

    barrier = pltpu.get_barrier_semaphore()
    near = ((has_prev, (tm - 1, row)), (has_next, (tm + 1, row)), (has_up, (tm, row - 1)), (has_down, (tm, row + 1)))
    expected = jnp.int32(21)
    for there, device in near:
        @pl.when(there)
        def _():
            pl.semaphore_signal(barrier, inc=1, device_id=device, device_id_type=MESH)
        expected = expected + there.astype(jnp.int32)
    for me, peer in ((a_me, a_peer), (y_me, y_peer), (z_me, z_peer)):
        for k in range(1, 8):
            pl.semaphore_signal(barrier, inc=1, device_id=peer((me + k) % 8), device_id_type=MESH)

    loads = [pltpu.make_async_copy(lat_hbm, win.at[:, 1:7], load_sem.at[0])]
    loads += [pltpu.make_async_copy(w_hbm.at[dt], w.at[dt], load_sem.at[1 + dt]) for dt in range(3)]
    loads += [pltpu.make_async_copy(tgt_hbm, tgt, load_sem.at[4])]
    loads += [pltpu.make_async_copy(gain_hbm, gain_ref, load_sem.at[5])]
    for load in loads:
        load.start()
    blank = jnp.zeros((2, 80, 256), BF16)
    win[:, 0] = blank
    win[:, 7] = blank

    @pl.when(row == 0)
    def _():
        halo[0] = blank

    @pl.when(row == 15)
    def _():
        halo[1] = blank

    @pl.when(tm == 0)
    def _():
        zin[...] = jnp.zeros(zin.shape, BF16)
        zed[...] = jnp.zeros(zed.shape, BF16)

    def taps(dst, o, pairs):
        @pl.loop(0, 3)
        def _(dw):
            cols = pl.ds(pl.multiple_of(dw * 256, 256), 256)
            acc = None
            for frame, dt in pairs:
                for dh in range(3):
                    piece = win[frame, dh : dh + 6].reshape(480, 256)
                    prod = jnp.dot(piece, w[dt, dh, cols], preferred_element_type=F32)
                    acc = prod if acc is None else acc + prod
            dst[o, dw] = acc

    def joined(src, o, rows, size):
        col = lax.broadcasted_iota(jnp.int32, (size, 1), 0) % 80
        left = jnp.where(col == 0, 0.0, pltpu.roll(src[o, 0, rows], 1, 0))
        right = jnp.where(col == 79, 0.0, pltpu.roll(src[o, 2, rows], size - 1, 0))
        return src[o, 1, rows] + left + right

    loads[0].wait()
    for f in (1, 0):
        loads[2 - f].wait()
        taps(nxt, f, NEXT[f])
        zin_out[f] = joined(nxt, f, pl.ds(80, 320), 320).astype(BF16).reshape(4, 80, 256)
    pl.semaphore_wait(barrier, expected)

    def side_copy(to):
        return pltpu.make_async_remote_copy(
            src_ref=win.at[:, 6 - 5 * to], dst_ref=halo.at[to], send_sem=side_send.at[to], recv_sem=side_recv.at[to],
            device_id=(tm, row + 1 - 2 * to), device_id_type=MESH,
        )

    def inner_copy(f):
        return pltpu.make_async_remote_copy(
            src_ref=zin_out.at[f], dst_ref=zin.at[f], send_sem=z_send.at[f], recv_sem=z_recv.at[f],
            device_id=(tm + 1, row), device_id_type=MESH,
        )

    def edge_copy(side):
        return pltpu.make_async_remote_copy(
            src_ref=zed_out.at[side], dst_ref=zed.at[side], send_sem=z_send.at[2 + side], recv_sem=z_recv.at[2 + side],
            device_id=(tm + 1, row), device_id_type=MESH,
        )

    @pl.when(has_down)
    def _():
        side_copy(0).start()

    @pl.when(has_up)
    def _():
        side_copy(1).start()

    @pl.when(has_next)
    def _():
        inner_copy(1).start()
        inner_copy(0).start()

    loads[3].wait()
    for f in range(2):
        taps(own, f, OWN[f])
        conv_in[f] = joined(own, f, pl.ds(80, 320), 320)

    def side_step(i, carry):
        side = (1 - core) * (1 - i) + core * i
        other = row + 2 * side - 1

        @pl.when((other >= 0) & (other <= 15))
        def _():
            side_copy(side).wait_recv()

        dh = 2 * side
        rows = pl.ds(pl.multiple_of(side * 400, 80), 80)

        @pl.loop(0, 3)
        def _(dw):
            cols = pl.ds(pl.multiple_of(dw * 256, 256), 256)
            both = halo[side].reshape(160, 256)
            p0 = jnp.dot(both, w[0, dh, cols], preferred_element_type=F32)
            p1 = jnp.dot(both[80:160], w[1, dh, cols], preferred_element_type=F32)
            nxt[0, dw, rows] += p0[0:80] + p1
            nxt[1, dw, rows] += p0[80:160]

        for f in range(2):
            zed_out[side, f] = joined(nxt, f, rows, 80).astype(BF16)

        @pl.when(has_next)
        def _():
            edge_copy(side).start()

        @pl.loop(0, 3)
        def _(dw):
            cols = pl.ds(pl.multiple_of(dw * 256, 256), 256)
            both = halo[side].reshape(160, 256)
            p0 = jnp.dot(both, w[2, dh, cols], preferred_element_type=F32)
            p1 = jnp.dot(both[0:80], w[1, dh, cols], preferred_element_type=F32)
            own[0, dw, rows] += p0[0:80]
            own[1, dw, rows] += p0[80:160] + p1

        for f in range(2):
            conv_edge[side, f] = joined(own, f, rows, 80)
        return carry

    lax.fori_loop(0, 2, side_step, 0)
    loads[4].wait()
    loads[5].wait()

    def finish(conv, base, target, first):
        size = conv.shape[0]
        mean = jnp.mean(conv * conv, axis=1, keepdims=True)
        v = conv * lax.rsqrt(mean + 1e-06) * gain_ref[...][None, :]
        out = (base.reshape(size, 256).astype(F32) + v / (1.0 + jnp.exp(-v))).astype(BF16)
        dims = (((0,), (0,)), ((), ()))
        g = lax.dot_general(out, out, dims, preferred_element_type=F32)
        c = lax.dot_general(out, target.reshape(size, 128), dims, preferred_element_type=F32)
        blocks = (g[0:128, 0:128], g[0:128, 128:256], g[128:256, 128:256], c[0:128], c[128:256])
        for i, block in enumerate(blocks):
            place = slice(128 * i, 128 * i + 128)
            sums[place] = block if first else sums[place] + block
        return out

    for f in (1, 0):
        @pl.when(has_prev)
        def _():
            inner_copy(f).wait_recv()

        conv = conv_in[f] + zin[f].reshape(320, 256).astype(F32)
        feat[f, 1:5] = finish(conv, win[f, 2:6], tgt[f, 1:5], f == 1).reshape(4, 80, 256)
    for side in range(2):
        @pl.when(has_prev)
        def _():
            edge_copy(side).wait_recv()

    conv = (conv_edge[...] + zed[...].astype(F32)).reshape(320, 256)
    base = jnp.concatenate([win[:, 1], win[:, 6]], axis=0)
    target = jnp.concatenate([tgt[:, 0], tgt[:, 5]], axis=0)
    out = finish(conv, base, target, False).reshape(2, 2, 80, 256)
    feat[:, 0] = out[0]
    feat[:, 5] = out[1]

    def copy(stage, me, peer, k, src, dst):
        j = (me + k) % 8
        return pltpu.make_async_remote_copy(
            src_ref=src(j), dst_ref=dst(me), send_sem=send_sem.at[stage, j], recv_sem=recv_sem.at[stage, me],
            device_id=peer(j), device_id_type=MESH,
        )

    def arrival(stage, me, peer, k, src, dst):
        j = (me + k) % 8
        return pltpu.make_async_remote_copy(
            src_ref=src(j), dst_ref=dst(j), send_sem=send_sem.at[stage, j], recv_sem=recv_sem.at[stage, j],
            device_id=peer(j), device_id_type=MESH,
        )

    def send(stage, me, peer, src, dst):
        for k in FAR:
            copy(stage, me, peer, k, src, dst).start()

    def receive(stage, me, peer, src, dst):
        for k in FAR:
            arrival(stage, me, peer, k, src, dst).wait_recv()

    def drain(stage, me, peer, src, dst):
        for k in FAR:
            copy(stage, me, peer, k, src, dst).wait_send()

    def chunk(ref, size):
        return lambda j: ref.at[pl.ds(pl.multiple_of(j * size, 8), size)]

    def slot(ref):
        return lambda j: ref.at[j]

    def total(ref):
        acc = ref[0].astype(F32)
        for j in range(1, 8):
            acc = acc + ref[j].astype(F32)
        return acc

    gpay[...] = sums[0:384].astype(BF16)
    gplace = pl.ds(pl.multiple_of(a_me * 48, 16), 48)
    cplace = pl.ds(pl.multiple_of(384 + a_me * 32, 8), 32)
    s0 = (0, a_me, a_peer, chunk(gpay, 48), slot(grs))
    s1 = (1, a_me, a_peer, lambda j: sums.at[pl.ds(pl.multiple_of(384 + j * 32, 8), 32)], slot(crs))
    send(*s0)
    send(*s1)
    grs[a_me] = gpay[gplace]
    crs[a_me] = sums[cplace]
    receive(*s0)
    ya[y_me] = total(grs).astype(BF16)
    s2 = (2, y_me, y_peer, lambda j: ya.at[y_me], slot(ya))
    send(*s2)
    receive(*s1)
    za[z_me] = total(crs)
    s3 = (3, z_me, z_peer, lambda j: za.at[z_me], slot(za))
    send(*s3)
    receive(*s2)
    zb[z_me] = total(ya).astype(BF16)
    s4 = (4, z_me, z_peer, lambda j: zb.at[z_me], slot(zb))
    send(*s4)
    receive(*s3)
    yb[y_me] = total(za)
    s5 = (5, y_me, y_peer, lambda j: yb.at[y_me], slot(yb))
    send(*s5)
    receive(*s4)
    fin[pl.ds(pl.multiple_of(a_me * 48, 16), 48)] = total(zb)
    s6 = (6, a_me, a_peer, lambda j: fin.at[gplace], chunk(fin, 48))
    send(*s6)
    receive(*s5)
    fin[cplace] = total(yb)
    s7 = (7, a_me, a_peer, lambda j: fin.at[cplace], lambda j: fin.at[pl.ds(pl.multiple_of(384 + j * 32, 8), 32)])
    send(*s7)
    receive(*s6)
    receive(*s7)

    for s in (s0, s1, s2, s3, s4, s5, s6, s7):
        drain(*s)

    @pl.when(has_down)
    def _():
        side_copy(0).wait_send()

    @pl.when(has_up)
    def _():
        side_copy(1).wait_send()

    @pl.when(has_next)
    def _():
        for i in range(2):
            inner_copy(i).wait_send()
            edge_copy(i).wait_send()


def write_kernel(scale, feat, fin, feat_out, gram_out, cross_out, gram, cross, sem):
    first = pltpu.make_async_copy(feat, feat_out, sem.at[0])
    first.start()
    cross[...] = fin[384:640] * scale
    second = pltpu.make_async_copy(cross, cross_out, sem.at[1])
    second.start()
    gram[0:128, 0:128] = fin[0:128] * scale
    gram[0:128, 128:256] = fin[128:256] * scale
    gram[128:256, 0:128] = fin[128:256].T * scale
    gram[128:256, 128:256] = fin[256:384] * scale
    third = pltpu.make_async_copy(gram, gram_out, sem.at[2])
    third.start()
    first.wait()
    second.wait()
    third.wait()


def on_device(latents, conv_weight, norm_gain, depth_target):
    vmem = pl.BlockSpec(memory_space=pltpu.VMEM)
    anywhere = pl.BlockSpec(memory_space=pltpu.HBM)
    dma = pltpu.SemaphoreType.DMA
    feat, fin = pl.pallas_call(
        layer_kernel,
        out_shape=(jax.ShapeDtypeStruct((2, 6, 80, 256), BF16), jax.ShapeDtypeStruct((640, 128), F32)),
        in_specs=[anywhere, anywhere, anywhere, anywhere],
        out_specs=(vmem, vmem),
        scratch_shapes=[
            pltpu.VMEM((2, 8, 80, 256), BF16),
            pltpu.VMEM((3, 3, 768, 256), BF16),
            pltpu.VMEM((2, 6, 80, 128), BF16),
            pltpu.VMEM((256,), F32),
            pltpu.VMEM((2, 3, 480, 256), F32),
            pltpu.VMEM((2, 3, 480, 256), F32),
            pltpu.VMEM((2, 2, 80, 256), BF16),
            pltpu.VMEM((2, 320, 256), F32),
            pltpu.VMEM((2, 2, 80, 256), F32),
            pltpu.VMEM((2, 4, 80, 256), BF16),
            pltpu.VMEM((2, 4, 80, 256), BF16),
            pltpu.VMEM((2, 2, 80, 256), BF16),
            pltpu.VMEM((2, 2, 80, 256), BF16),
            pltpu.VMEM((640, 128), F32),
            pltpu.VMEM((384, 128), BF16),
            pltpu.VMEM((8, 48, 128), BF16),
            pltpu.VMEM((8, 32, 128), F32),
            pltpu.VMEM((8, 48, 128), BF16),
            pltpu.VMEM((8, 32, 128), F32),
            pltpu.VMEM((8, 32, 128), F32),
            pltpu.VMEM((8, 48, 128), BF16),
            dma((6,)),
            dma((2,)),
            dma((2,)),
            dma((4,)),
            dma((4,)),
            dma((8, 8)),
            dma((8, 8)),
        ],
        compiler_params=pltpu.CompilerParams(collective_id=0, has_side_effects=True, vmem_limit_bytes=40 << 20),
    )(*(pltpu.with_memory_space_constraint(a, pltpu.HBM) for a in (latents, conv_weight, norm_gain, depth_target)))
    count = 960 * lax.axis_size("tm") * lax.axis_size("row")
    return pl.pallas_call(
        functools.partial(write_kernel, 1.0 / count),
        out_shape=(
            jax.ShapeDtypeStruct((2, 6, 80, 256), BF16),
            jax.ShapeDtypeStruct((256, 256), F32),
            jax.ShapeDtypeStruct((256, 128), F32),
        ),
        in_specs=[vmem, vmem],
        out_specs=(anywhere, anywhere, anywhere),
        scratch_shapes=[pltpu.VMEM((256, 256), F32), pltpu.VMEM((256, 128), F32), dma((3,))],
        compiler_params=pltpu.CompilerParams(vmem_limit_bytes=40 << 20),
    )(feat, fin)


def solution(mesh):
    in_specs = (P("tm", "row", None, None), P(), P(), P("tm", "row", None, None))
    out_specs = (P("tm", "row", None, None), P(), P())
    return jax.shard_map(
        on_device, mesh=mesh, in_specs=in_specs, out_specs=out_specs, check_vma=False
    )
```

```python
import functools

import jax
import jax.numpy as jnp
from jax import lax
from jax.experimental import pallas as pl
from jax.experimental.pallas import tpu as pltpu
from jax.sharding import PartitionSpec as P

MESH = pl.DeviceIdType.MESH
FAR = (4, 3, 5, 2, 6, 1, 7)
F32, BF16 = jnp.float32, jnp.bfloat16
OWN = (((0, 2),), ((0, 1), (1, 2)))
NEXT = (((0, 0), (1, 1)), ((1, 0),))


def layer_kernel(
    lat_hbm, w_hbm, gain_hbm, tgt_hbm, feat, fin,
    win, w, tgt, gain_ref, own, nxt, halo, conv_in, conv_edge, zin_out, zin, zed_out, zed,
    sums, gpay, grs, crs, ya, za, yb, zb, load_sem, side_send, side_recv, z_send, z_recv, send_sem, recv_sem,
):
    tm = lax.axis_index("tm")
    row = lax.axis_index("row")
    y, zl = tm // 4, tm % 4
    x, zh, core = row // 4, (row // 2) % 2, row % 2

    def a_peer(j):
        return tm, (j // 2) * 4 + zh * 2 + j % 2

    def y_peer(j):
        return j * 4 + zl, row

    def z_peer(j):
        return y * 4 + j % 4, x * 4 + (j // 4) * 2 + core

    a_me, y_me, z_me = x * 2 + core, y, zh * 4 + zl
    has_prev, has_next, has_up, has_down = tm > 0, tm < 31, row > 0, row < 15

    barrier = pltpu.get_barrier_semaphore()
    near = ((has_prev, (tm - 1, row)), (has_next, (tm + 1, row)), (has_up, (tm, row - 1)), (has_down, (tm, row + 1)))
    expected = jnp.int32(21)
    for there, device in near:
        @pl.when(there)
        def _():
            pl.semaphore_signal(barrier, inc=1, device_id=device, device_id_type=MESH)
        expected = expected + there.astype(jnp.int32)
    for me, peer in ((a_me, a_peer), (y_me, y_peer), (z_me, z_peer)):
        for k in range(1, 8):
            pl.semaphore_signal(barrier, inc=1, device_id=peer((me + k) % 8), device_id_type=MESH)

    loads = [pltpu.make_async_copy(lat_hbm, win.at[:, 1:7], load_sem.at[0])]
    loads += [pltpu.make_async_copy(w_hbm.at[dt], w.at[dt], load_sem.at[1 + dt]) for dt in range(3)]
    loads += [pltpu.make_async_copy(tgt_hbm, tgt, load_sem.at[4])]
    loads += [pltpu.make_async_copy(gain_hbm, gain_ref, load_sem.at[5])]
    for load in loads:
        load.start()
    blank = jnp.zeros((2, 80, 256), BF16)
    win[:, 0] = blank
    win[:, 7] = blank

    @pl.when(row == 0)
    def _():
        halo[0] = blank

    @pl.when(row == 15)
    def _():
        halo[1] = blank

    @pl.when(tm == 0)
    def _():
        zin[...] = jnp.zeros(zin.shape, BF16)
        zed[...] = jnp.zeros(zed.shape, BF16)

    def taps(dst, o, pairs):
        @pl.loop(0, 3)
        def _(dw):
            cols = pl.ds(pl.multiple_of(dw * 256, 256), 256)
            acc = None
            for frame, dt in pairs:
                for dh in range(3):
                    piece = win[frame, dh : dh + 6].reshape(480, 256)
                    prod = jnp.dot(piece, w[dt, dh, cols], preferred_element_type=F32)
                    acc = prod if acc is None else acc + prod
            dst[o, dw] = acc

    def joined(src, o, rows, size):
        col = lax.broadcasted_iota(jnp.int32, (size, 1), 0) % 80
        left = jnp.where(col == 0, 0.0, pltpu.roll(src[o, 0, rows], 1, 0))
        right = jnp.where(col == 79, 0.0, pltpu.roll(src[o, 2, rows], size - 1, 0))
        return src[o, 1, rows] + left + right

    loads[0].wait()
    pl.semaphore_wait(barrier, expected)

    def side_copy(to):
        return pltpu.make_async_remote_copy(
            src_ref=win.at[:, 6 - 5 * to], dst_ref=halo.at[to], send_sem=side_send.at[to], recv_sem=side_recv.at[to],
            device_id=(tm, row + 1 - 2 * to), device_id_type=MESH,
        )

    def inner_copy(f):
        return pltpu.make_async_remote_copy(
            src_ref=zin_out.at[f], dst_ref=zin.at[f], send_sem=z_send.at[f], recv_sem=z_recv.at[f],
            device_id=(tm + 1, row), device_id_type=MESH,
        )

    def edge_copy(side):
        return pltpu.make_async_remote_copy(
            src_ref=zed_out.at[side], dst_ref=zed.at[side], send_sem=z_send.at[2 + side], recv_sem=z_recv.at[2 + side],
            device_id=(tm + 1, row), device_id_type=MESH,
        )

    @pl.when(has_down)
    def _():
        side_copy(0).start()

    @pl.when(has_up)
    def _():
        side_copy(1).start()

    for f in (1, 0):
        loads[2 - f].wait()
        taps(nxt, f, NEXT[f])
        zin_out[f] = joined(nxt, f, pl.ds(80, 320), 320).astype(BF16).reshape(4, 80, 256)

        @pl.when(has_next)
        def _():
            inner_copy(f).start()

    def edge_rows(side):
        return pl.ds(pl.multiple_of(side * 400, 80), 80)

    def edge_next(side):
        other = row + 2 * side - 1

        @pl.when((other >= 0) & (other <= 15))
        def _():
            side_copy(side).wait_recv()

        dh = 2 * side
        rows = edge_rows(side)

        @pl.loop(0, 3)
        def _(dw):
            cols = pl.ds(pl.multiple_of(dw * 256, 256), 256)
            both = halo[side].reshape(160, 256)
            p0 = jnp.dot(both, w[0, dh, cols], preferred_element_type=F32)
            p1 = jnp.dot(both[80:160], w[1, dh, cols], preferred_element_type=F32)
            nxt[0, dw, rows] += p0[0:80] + p1
            nxt[1, dw, rows] += p0[80:160]

        for f in range(2):
            zed_out[side, f] = joined(nxt, f, rows, 80).astype(BF16)

        @pl.when(has_next)
        def _():
            edge_copy(side).start()

    near_side, far_side = 1 - core, core
    edge_next(near_side)

    loads[3].wait()
    for f in range(2):
        taps(own, f, OWN[f])
        conv_in[f] = joined(own, f, pl.ds(80, 320), 320)
    edge_next(far_side)

    def edge_own(side, carry):
        dh = 2 * side
        rows = edge_rows(side)

        @pl.loop(0, 3)
        def _(dw):
            cols = pl.ds(pl.multiple_of(dw * 256, 256), 256)
            both = halo[side].reshape(160, 256)
            p0 = jnp.dot(both, w[2, dh, cols], preferred_element_type=F32)
            p1 = jnp.dot(both[0:80], w[1, dh, cols], preferred_element_type=F32)
            own[0, dw, rows] += p0[0:80]
            own[1, dw, rows] += p0[80:160] + p1

        for f in range(2):
            conv_edge[side, f] = joined(own, f, rows, 80)
        return carry

    lax.fori_loop(0, 2, edge_own, 0)
    loads[4].wait()
    loads[5].wait()

    def finish(conv, base, target, first):
        size = conv.shape[0]
        mean = jnp.mean(conv * conv, axis=1, keepdims=True)
        v = conv * lax.rsqrt(mean + 1e-06) * gain_ref[...][None, :]
        out = (base.reshape(size, 256).astype(F32) + v / (1.0 + jnp.exp(-v))).astype(BF16)
        dims = (((0,), (0,)), ((), ()))
        g = lax.dot_general(out, out, dims, preferred_element_type=F32)
        c = lax.dot_general(out, target.reshape(size, 128), dims, preferred_element_type=F32)
        blocks = (g[0:128, 0:128], g[0:128, 128:256], g[128:256, 128:256], c[0:128], c[128:256])
        for i, block in enumerate(blocks):
            place = slice(128 * i, 128 * i + 128)
            sums[place] = block if first else sums[place] + block
        return out

    for f in (1, 0):
        @pl.when(has_prev)
        def _():
            inner_copy(f).wait_recv()

        conv = conv_in[f] + zin[f].reshape(320, 256).astype(F32)
        feat[f, 1:5] = finish(conv, win[f, 2:6], tgt[f, 1:5], f == 1).reshape(4, 80, 256)
    for side in (near_side, far_side):
        @pl.when(has_prev)
        def _():
            edge_copy(side).wait_recv()

        conv = (conv_edge[side] + zed[side].astype(F32)).reshape(160, 256)
        out = finish(conv, win[:, 1 + 5 * side], tgt[:, 5 * side], False)
        feat[:, 5 * side] = out.reshape(2, 80, 256)

    def copy(stage, me, peer, k, src, dst):
        j = (me + k) % 8
        return pltpu.make_async_remote_copy(
            src_ref=src(j), dst_ref=dst(me), send_sem=send_sem.at[stage, j], recv_sem=recv_sem.at[stage, me],
            device_id=peer(j), device_id_type=MESH,
        )

    def arrival(stage, me, peer, k, src, dst):
        j = (me + k) % 8
        return pltpu.make_async_remote_copy(
            src_ref=src(j), dst_ref=dst(j), send_sem=send_sem.at[stage, j], recv_sem=recv_sem.at[stage, j],
            device_id=peer(j), device_id_type=MESH,
        )

    def send(stage, me, peer, src, dst):
        for k in FAR:
            copy(stage, me, peer, k, src, dst).start()

    def receive(stage, me, peer, src, dst):
        for k in FAR:
            arrival(stage, me, peer, k, src, dst).wait_recv()

    def drain(stage, me, peer, src, dst):
        for k in FAR:
            copy(stage, me, peer, k, src, dst).wait_send()

    def chunk(ref, size):
        return lambda j: ref.at[pl.ds(pl.multiple_of(j * size, 8), size)]

    def slot(ref):
        return lambda j: ref.at[j]

    def total(ref):
        acc = ref[0].astype(F32)
        for j in range(1, 8):
            acc = acc + ref[j].astype(F32)
        return acc

    gpay[...] = sums[0:384].astype(BF16)
    gplace = pl.ds(pl.multiple_of(a_me * 48, 16), 48)
    cplace = pl.ds(pl.multiple_of(384 + a_me * 32, 8), 32)
    s0 = (0, a_me, a_peer, chunk(gpay, 48), slot(grs))
    s1 = (1, a_me, a_peer, lambda j: sums.at[pl.ds(pl.multiple_of(384 + j * 32, 8), 32)], slot(crs))
    send(*s0)
    send(*s1)
    grs[a_me] = gpay[gplace]
    crs[a_me] = sums[cplace]
    receive(*s0)
    ya[y_me] = total(grs).astype(BF16)
    s2 = (2, y_me, y_peer, lambda j: ya.at[y_me], slot(ya))
    send(*s2)
    receive(*s1)
    za[z_me] = total(crs)
    s3 = (3, z_me, z_peer, lambda j: za.at[z_me], slot(za))
    send(*s3)
    receive(*s2)
    zb[z_me] = total(ya).astype(BF16)
    s4 = (4, z_me, z_peer, lambda j: zb.at[z_me], slot(zb))
    send(*s4)
    receive(*s3)
    yb[y_me] = total(za)
    s5 = (5, y_me, y_peer, lambda j: yb.at[y_me], slot(yb))
    send(*s5)
    receive(*s4)
    fin[pl.ds(pl.multiple_of(a_me * 48, 16), 48)] = total(zb)
    s6 = (6, a_me, a_peer, lambda j: fin.at[gplace], chunk(fin, 48))
    send(*s6)
    receive(*s5)
    fin[cplace] = total(yb)
    s7 = (7, a_me, a_peer, lambda j: fin.at[cplace], lambda j: fin.at[pl.ds(pl.multiple_of(384 + j * 32, 8), 32)])
    send(*s7)
    receive(*s6)
    receive(*s7)

    for s in (s0, s1, s2, s3, s4, s5, s6, s7):
        drain(*s)

    @pl.when(has_down)
    def _():
        side_copy(0).wait_send()

    @pl.when(has_up)
    def _():
        side_copy(1).wait_send()

    @pl.when(has_next)
    def _():
        for i in range(2):
            inner_copy(i).wait_send()
            edge_copy(i).wait_send()


def write_kernel(scale, feat, fin, feat_out, gram_out, cross_out, gram, cross, sem):
    first = pltpu.make_async_copy(feat, feat_out, sem.at[0])
    first.start()
    cross[...] = fin[384:640] * scale
    second = pltpu.make_async_copy(cross, cross_out, sem.at[1])
    second.start()
    gram[0:128, 0:128] = fin[0:128] * scale
    gram[0:128, 128:256] = fin[128:256] * scale
    gram[128:256, 0:128] = fin[128:256].T * scale
    gram[128:256, 128:256] = fin[256:384] * scale
    third = pltpu.make_async_copy(gram, gram_out, sem.at[2])
    third.start()
    first.wait()
    second.wait()
    third.wait()


def on_device(latents, conv_weight, norm_gain, depth_target):
    vmem = pl.BlockSpec(memory_space=pltpu.VMEM)
    anywhere = pl.BlockSpec(memory_space=pltpu.HBM)
    dma = pltpu.SemaphoreType.DMA
    feat, fin = pl.pallas_call(
        layer_kernel,
        out_shape=(jax.ShapeDtypeStruct((2, 6, 80, 256), BF16), jax.ShapeDtypeStruct((640, 128), F32)),
        in_specs=[anywhere, anywhere, anywhere, anywhere],
        out_specs=(vmem, vmem),
        scratch_shapes=[
            pltpu.VMEM((2, 8, 80, 256), BF16),
            pltpu.VMEM((3, 3, 768, 256), BF16),
            pltpu.VMEM((2, 6, 80, 128), BF16),
            pltpu.VMEM((256,), F32),
            pltpu.VMEM((2, 3, 480, 256), F32),
            pltpu.VMEM((2, 3, 480, 256), F32),
            pltpu.VMEM((2, 2, 80, 256), BF16),
            pltpu.VMEM((2, 320, 256), F32),
            pltpu.VMEM((2, 2, 80, 256), F32),
            pltpu.VMEM((2, 4, 80, 256), BF16),
            pltpu.VMEM((2, 4, 80, 256), BF16),
            pltpu.VMEM((2, 2, 80, 256), BF16),
            pltpu.VMEM((2, 2, 80, 256), BF16),
            pltpu.VMEM((640, 128), F32),
            pltpu.VMEM((384, 128), BF16),
            pltpu.VMEM((8, 48, 128), BF16),
            pltpu.VMEM((8, 32, 128), F32),
            pltpu.VMEM((8, 48, 128), BF16),
            pltpu.VMEM((8, 32, 128), F32),
            pltpu.VMEM((8, 32, 128), F32),
            pltpu.VMEM((8, 48, 128), BF16),
            dma((6,)),
            dma((2,)),
            dma((2,)),
            dma((4,)),
            dma((4,)),
            dma((8, 8)),
            dma((8, 8)),
        ],
        compiler_params=pltpu.CompilerParams(collective_id=0, has_side_effects=True, vmem_limit_bytes=40 << 20),
    )(*(pltpu.with_memory_space_constraint(a, pltpu.HBM) for a in (latents, conv_weight, norm_gain, depth_target)))
    count = 960 * lax.axis_size("tm") * lax.axis_size("row")
    return pl.pallas_call(
        functools.partial(write_kernel, 1.0 / count),
        out_shape=(
            jax.ShapeDtypeStruct((2, 6, 80, 256), BF16),
            jax.ShapeDtypeStruct((256, 256), F32),
            jax.ShapeDtypeStruct((256, 128), F32),
        ),
        in_specs=[vmem, vmem],
        out_specs=(anywhere, anywhere, anywhere),
        scratch_shapes=[pltpu.VMEM((256, 256), F32), pltpu.VMEM((256, 128), F32), dma((3,))],
        compiler_params=pltpu.CompilerParams(vmem_limit_bytes=40 << 20),
    )(feat, fin)


def solution(mesh):
    in_specs = (P("tm", "row", None, None), P(), P(), P("tm", "row", None, None))
    out_specs = (P("tm", "row", None, None), P(), P())
    return jax.shard_map(
        on_device, mesh=mesh, in_specs=in_specs, out_specs=out_specs, check_vma=False
    )
```

```python
import functools

import jax
import jax.numpy as jnp
from jax import lax
from jax.experimental import pallas as pl
from jax.experimental.pallas import tpu as pltpu
from jax.sharding import PartitionSpec as P

MESH = pl.DeviceIdType.MESH
FAR = (4, 3, 5, 2, 6, 1, 7)
F32, BF16 = jnp.float32, jnp.bfloat16
OWN = (((0, 2),), ((0, 1), (1, 2)))
NEXT = (((0, 0), (1, 1)), ((1, 0),))


def layer_kernel(
    lat_hbm, w_hbm, gain_hbm, tgt_hbm, feat, fin,
    win, w, tgt, gain_ref, own, nxt, halo, passing, conv_in, conv_edge, zin_out, zin, zed_out, zed,
    sums, gpay, grs, crs, ya, za, yb, zb, load_sem, side_send, side_recv, relay_sem, z_send, z_recv, send_sem, recv_sem,
):
    tm = lax.axis_index("tm")
    row = lax.axis_index("row")
    y, zl = tm // 4, tm % 4
    x, zh, core = row // 4, (row // 2) % 2, row % 2

    def a_peer(j):
        return tm, (j // 2) * 4 + zh * 2 + j % 2

    def y_peer(j):
        return j * 4 + zl, row

    def z_peer(j):
        return y * 4 + j % 4, x * 4 + (j // 4) * 2 + core

    a_me, y_me, z_me = x * 2 + core, y, zh * 4 + zl
    has_prev, has_next, has_up, has_down = tm > 0, tm < 31, row > 0, row < 15

    z = zh * 4 + zl

    def ring(zz, xx):
        return y * 4 + zz % 4, xx * 4 + (zz // 4) * 2

    relay = ring((z + 6) % 8, x)
    origin_tm, origin_row = ring((z + 2) % 8, x)
    relays = (core == 0) & (origin_row > 0)
    relayed_by = ring(((((row + 1) // 2) % 2) * 4 + zl + 6) % 8, (row + 1) // 4)

    barrier = pltpu.get_barrier_semaphore()
    near = ((has_prev, (tm - 1, row)), (has_next, (tm + 1, row)), (has_up, (tm, row - 1)), (has_down, (tm, row + 1)))
    expected = jnp.int32(21)
    for there, device in near:
        @pl.when(there)
        def _():
            pl.semaphore_signal(barrier, inc=1, device_id=device, device_id_type=MESH)
        expected = expected + there.astype(jnp.int32)
    @pl.when((core == 1) & has_down)
    def _():
        pl.semaphore_signal(barrier, inc=1, device_id=relayed_by, device_id_type=MESH)

    expected = expected + relays.astype(jnp.int32)
    for me, peer in ((a_me, a_peer), (y_me, y_peer), (z_me, z_peer)):
        for k in range(1, 8):
            pl.semaphore_signal(barrier, inc=1, device_id=peer((me + k) % 8), device_id_type=MESH)

    loads = [pltpu.make_async_copy(lat_hbm, win.at[:, 1:7], load_sem.at[0])]
    loads += [pltpu.make_async_copy(w_hbm.at[dt], w.at[dt], load_sem.at[1 + dt]) for dt in range(3)]
    loads += [pltpu.make_async_copy(tgt_hbm, tgt, load_sem.at[4])]
    loads += [pltpu.make_async_copy(gain_hbm, gain_ref, load_sem.at[5])]
    for load in loads:
        load.start()
    blank = jnp.zeros((2, 80, 256), BF16)
    win[:, 0] = blank
    win[:, 7] = blank

    @pl.when(row == 0)
    def _():
        halo[0] = blank

    @pl.when(row == 15)
    def _():
        halo[1] = blank

    @pl.when(tm == 0)
    def _():
        zin[...] = jnp.zeros(zin.shape, BF16)
        zed[...] = jnp.zeros(zed.shape, BF16)

    def taps(dst, o, pairs):
        @pl.loop(0, 3)
        def _(dw):
            cols = pl.ds(pl.multiple_of(dw * 256, 256), 256)
            acc = None
            for frame, dt in pairs:
                for dh in range(3):
                    piece = win[frame, dh : dh + 6].reshape(480, 256)
                    prod = jnp.dot(piece, w[dt, dh, cols], preferred_element_type=F32)
                    acc = prod if acc is None else acc + prod
            dst[o, dw] = acc

    def joined(src, o, rows, size):
        col = lax.broadcasted_iota(jnp.int32, (size, 1), 0) % 80
        left = jnp.where(col == 0, 0.0, pltpu.roll(src[o, 0, rows], 1, 0))
        right = jnp.where(col == 79, 0.0, pltpu.roll(src[o, 2, rows], size - 1, 0))
        return src[o, 1, rows] + left + right

    loads[0].wait()
    pl.semaphore_wait(barrier, expected)

    def side_copy(to):
        return pltpu.make_async_remote_copy(
            src_ref=win.at[:, 6 - 5 * to], dst_ref=halo.at[to], send_sem=side_send.at[to], recv_sem=side_recv.at[to],
            device_id=(tm, row + 1 - 2 * to), device_id_type=MESH,
        )

    def inner_copy(f):
        return pltpu.make_async_remote_copy(
            src_ref=zin_out.at[f], dst_ref=zin.at[f], send_sem=z_send.at[f], recv_sem=z_recv.at[f],
            device_id=(tm + 1, row), device_id_type=MESH,
        )

    def edge_copy(side):
        return pltpu.make_async_remote_copy(
            src_ref=zed_out.at[side], dst_ref=zed.at[side], send_sem=z_send.at[2 + side], recv_sem=z_recv.at[2 + side],
            device_id=(tm + 1, row), device_id_type=MESH,
        )

    @pl.when(has_down)
    def _():
        side_copy(0).start()

    def relay_in():
        return pltpu.make_async_remote_copy(
            src_ref=win.at[:, 1], dst_ref=passing, send_sem=side_send.at[1], recv_sem=relay_sem.at[0],
            device_id=relay, device_id_type=MESH,
        )

    def relay_out():
        return pltpu.make_async_remote_copy(
            src_ref=passing, dst_ref=halo.at[1], send_sem=relay_sem.at[1], recv_sem=side_recv.at[1],
            device_id=(origin_tm, origin_row - 1), device_id_type=MESH,
        )

    @pl.when((core == 0) & has_up)
    def _():
        relay_in().start()

    @pl.when(core == 1)
    def _():
        side_copy(1).start()

    for f in (1, 0):
        loads[2 - f].wait()
        taps(nxt, f, NEXT[f])
        zin_out[f] = joined(nxt, f, pl.ds(80, 320), 320).astype(BF16).reshape(4, 80, 256)

        @pl.when(has_next)
        def _():
            inner_copy(f).start()

    def edge_rows(side):
        return pl.ds(pl.multiple_of(side * 400, 80), 80)

    def edge_next(side):
        other = row + 2 * side - 1

        @pl.when((other >= 0) & (other <= 15))
        def _():
            side_copy(side).wait_recv()

        dh = 2 * side
        rows = edge_rows(side)

        @pl.loop(0, 3)
        def _(dw):
            cols = pl.ds(pl.multiple_of(dw * 256, 256), 256)
            both = halo[side].reshape(160, 256)
            p0 = jnp.dot(both, w[0, dh, cols], preferred_element_type=F32)
            p1 = jnp.dot(both[80:160], w[1, dh, cols], preferred_element_type=F32)
            nxt[0, dw, rows] += p0[0:80] + p1
            nxt[1, dw, rows] += p0[80:160]

        for f in range(2):
            zed_out[side, f] = joined(nxt, f, rows, 80).astype(BF16)

        @pl.when(has_next)
        def _():
            edge_copy(side).start()

    near_side, far_side = 1 - core, core
    edge_next(near_side)

    @pl.when(relays)
    def _():
        relay_in().wait_recv()
        relay_out().start()

    loads[3].wait()
    for f in range(2):
        taps(own, f, OWN[f])
        conv_in[f] = joined(own, f, pl.ds(80, 320), 320)
    edge_next(far_side)

    def edge_own(side, carry):
        dh = 2 * side
        rows = edge_rows(side)

        @pl.loop(0, 3)
        def _(dw):
            cols = pl.ds(pl.multiple_of(dw * 256, 256), 256)
            both = halo[side].reshape(160, 256)
            p0 = jnp.dot(both, w[2, dh, cols], preferred_element_type=F32)
            p1 = jnp.dot(both[0:80], w[1, dh, cols], preferred_element_type=F32)
            own[0, dw, rows] += p0[0:80]
            own[1, dw, rows] += p0[80:160] + p1

        for f in range(2):
            conv_edge[side, f] = joined(own, f, rows, 80)
        return carry

    lax.fori_loop(0, 2, edge_own, 0)
    loads[4].wait()
    loads[5].wait()

    def finish(conv, base, target, first):
        size = conv.shape[0]
        mean = jnp.mean(conv * conv, axis=1, keepdims=True)
        v = conv * lax.rsqrt(mean + 1e-06) * gain_ref[...][None, :]
        out = (base.reshape(size, 256).astype(F32) + v / (1.0 + jnp.exp(-v))).astype(BF16)
        dims = (((0,), (0,)), ((), ()))
        g = lax.dot_general(out, out, dims, preferred_element_type=F32)
        c = lax.dot_general(out, target.reshape(size, 128), dims, preferred_element_type=F32)
        blocks = (g[0:128, 0:128], g[0:128, 128:256], g[128:256, 128:256], c[0:128], c[128:256])
        for i, block in enumerate(blocks):
            place = slice(128 * i, 128 * i + 128)
            sums[place] = block if first else sums[place] + block
        return out

    for f in (1, 0):
        @pl.when(has_prev)
        def _():
            inner_copy(f).wait_recv()

        conv = conv_in[f] + zin[f].reshape(320, 256).astype(F32)
        feat[f, 1:5] = finish(conv, win[f, 2:6], tgt[f, 1:5], f == 1).reshape(4, 80, 256)
    for side in (near_side, far_side):
        @pl.when(has_prev)
        def _():
            edge_copy(side).wait_recv()

        conv = (conv_edge[side] + zed[side].astype(F32)).reshape(160, 256)
        out = finish(conv, win[:, 1 + 5 * side], tgt[:, 5 * side], False)
        feat[:, 5 * side] = out.reshape(2, 80, 256)

    def copy(stage, me, peer, k, src, dst):
        j = (me + k) % 8
        return pltpu.make_async_remote_copy(
            src_ref=src(j), dst_ref=dst(me), send_sem=send_sem.at[stage, j], recv_sem=recv_sem.at[stage, me],
            device_id=peer(j), device_id_type=MESH,
        )

    def arrival(stage, me, peer, k, src, dst):
        j = (me + k) % 8
        return pltpu.make_async_remote_copy(
            src_ref=src(j), dst_ref=dst(j), send_sem=send_sem.at[stage, j], recv_sem=recv_sem.at[stage, j],
            device_id=peer(j), device_id_type=MESH,
        )

    def send(stage, me, peer, src, dst):
        for k in FAR:
            copy(stage, me, peer, k, src, dst).start()

    def receive(stage, me, peer, src, dst):
        for k in FAR:
            arrival(stage, me, peer, k, src, dst).wait_recv()

    def drain(stage, me, peer, src, dst):
        for k in FAR:
            copy(stage, me, peer, k, src, dst).wait_send()

    def chunk(ref, size):
        return lambda j: ref.at[pl.ds(pl.multiple_of(j * size, 8), size)]

    def slot(ref):
        return lambda j: ref.at[j]

    def total(ref):
        acc = ref[0].astype(F32)
        for j in range(1, 8):
            acc = acc + ref[j].astype(F32)
        return acc

    gpay[...] = sums[0:384].astype(BF16)
    gplace = pl.ds(pl.multiple_of(a_me * 48, 16), 48)
    cplace = pl.ds(pl.multiple_of(384 + a_me * 32, 8), 32)
    s0 = (0, a_me, a_peer, chunk(gpay, 48), slot(grs))
    s1 = (1, a_me, a_peer, lambda j: sums.at[pl.ds(pl.multiple_of(384 + j * 32, 8), 32)], slot(crs))
    send(*s0)
    send(*s1)
    grs[a_me] = gpay[gplace]
    crs[a_me] = sums[cplace]
    receive(*s0)
    ya[y_me] = total(grs).astype(BF16)
    s2 = (2, y_me, y_peer, lambda j: ya.at[y_me], slot(ya))
    send(*s2)
    receive(*s1)
    za[z_me] = total(crs)
    s3 = (3, z_me, z_peer, lambda j: za.at[z_me], slot(za))
    send(*s3)
    receive(*s2)
    zb[z_me] = total(ya).astype(BF16)
    s4 = (4, z_me, z_peer, lambda j: zb.at[z_me], slot(zb))
    send(*s4)
    receive(*s3)
    yb[y_me] = total(za)
    s5 = (5, y_me, y_peer, lambda j: yb.at[y_me], slot(yb))
    send(*s5)
    receive(*s4)
    fin[pl.ds(pl.multiple_of(a_me * 48, 16), 48)] = total(zb)
    s6 = (6, a_me, a_peer, lambda j: fin.at[gplace], chunk(fin, 48))
    send(*s6)
    receive(*s5)
    fin[cplace] = total(yb)
    s7 = (7, a_me, a_peer, lambda j: fin.at[cplace], lambda j: fin.at[pl.ds(pl.multiple_of(384 + j * 32, 8), 32)])
    send(*s7)
    receive(*s6)
    receive(*s7)

    for s in (s0, s1, s2, s3, s4, s5, s6, s7):
        drain(*s)

    @pl.when(has_down)
    def _():
        side_copy(0).wait_send()

    @pl.when(has_up)
    def _():
        side_copy(1).wait_send()

    @pl.when(relays)
    def _():
        relay_out().wait_send()

    @pl.when(has_next)
    def _():
        for i in range(2):
            inner_copy(i).wait_send()
            edge_copy(i).wait_send()


def write_kernel(scale, feat, fin, feat_out, gram_out, cross_out, gram, cross, sem):
    first = pltpu.make_async_copy(feat, feat_out, sem.at[0])
    first.start()
    cross[...] = fin[384:640] * scale
    second = pltpu.make_async_copy(cross, cross_out, sem.at[1])
    second.start()
    gram[0:128, 0:128] = fin[0:128] * scale
    gram[0:128, 128:256] = fin[128:256] * scale
    gram[128:256, 0:128] = fin[128:256].T * scale
    gram[128:256, 128:256] = fin[256:384] * scale
    third = pltpu.make_async_copy(gram, gram_out, sem.at[2])
    third.start()
    first.wait()
    second.wait()
    third.wait()


def on_device(latents, conv_weight, norm_gain, depth_target):
    vmem = pl.BlockSpec(memory_space=pltpu.VMEM)
    anywhere = pl.BlockSpec(memory_space=pltpu.HBM)
    dma = pltpu.SemaphoreType.DMA
    feat, fin = pl.pallas_call(
        layer_kernel,
        out_shape=(jax.ShapeDtypeStruct((2, 6, 80, 256), BF16), jax.ShapeDtypeStruct((640, 128), F32)),
        in_specs=[anywhere, anywhere, anywhere, anywhere],
        out_specs=(vmem, vmem),
        scratch_shapes=[
            pltpu.VMEM((2, 8, 80, 256), BF16),
            pltpu.VMEM((3, 3, 768, 256), BF16),
            pltpu.VMEM((2, 6, 80, 128), BF16),
            pltpu.VMEM((256,), F32),
            pltpu.VMEM((2, 3, 480, 256), F32),
            pltpu.VMEM((2, 3, 480, 256), F32),
            pltpu.VMEM((2, 2, 80, 256), BF16),
            pltpu.VMEM((2, 80, 256), BF16),
            pltpu.VMEM((2, 320, 256), F32),
            pltpu.VMEM((2, 2, 80, 256), F32),
            pltpu.VMEM((2, 4, 80, 256), BF16),
            pltpu.VMEM((2, 4, 80, 256), BF16),
            pltpu.VMEM((2, 2, 80, 256), BF16),
            pltpu.VMEM((2, 2, 80, 256), BF16),
            pltpu.VMEM((640, 128), F32),
            pltpu.VMEM((384, 128), BF16),
            pltpu.VMEM((8, 48, 128), BF16),
            pltpu.VMEM((8, 32, 128), F32),
            pltpu.VMEM((8, 48, 128), BF16),
            pltpu.VMEM((8, 32, 128), F32),
            pltpu.VMEM((8, 32, 128), F32),
            pltpu.VMEM((8, 48, 128), BF16),
            dma((6,)),
            dma((2,)),
            dma((2,)),
            dma((2,)),
            dma((4,)),
            dma((4,)),
            dma((8, 8)),
            dma((8, 8)),
        ],
        compiler_params=pltpu.CompilerParams(collective_id=0, has_side_effects=True, vmem_limit_bytes=40 << 20),
    )(*(pltpu.with_memory_space_constraint(a, pltpu.HBM) for a in (latents, conv_weight, norm_gain, depth_target)))
    count = 960 * lax.axis_size("tm") * lax.axis_size("row")
    return pl.pallas_call(
        functools.partial(write_kernel, 1.0 / count),
        out_shape=(
            jax.ShapeDtypeStruct((2, 6, 80, 256), BF16),
            jax.ShapeDtypeStruct((256, 256), F32),
            jax.ShapeDtypeStruct((256, 128), F32),
        ),
        in_specs=[vmem, vmem],
        out_specs=(anywhere, anywhere, anywhere),
        scratch_shapes=[pltpu.VMEM((256, 256), F32), pltpu.VMEM((256, 128), F32), dma((3,))],
        compiler_params=pltpu.CompilerParams(vmem_limit_bytes=40 << 20),
    )(feat, fin)


def solution(mesh):
    in_specs = (P("tm", "row", None, None), P(), P(), P("tm", "row", None, None))
    out_specs = (P("tm", "row", None, None), P(), P())
    return jax.shard_map(
        on_device, mesh=mesh, in_specs=in_specs, out_specs=out_specs, check_vma=False
    )
```

```python
import functools

import jax
import jax.numpy as jnp
from jax import lax
from jax.experimental import pallas as pl
from jax.experimental.pallas import tpu as pltpu
from jax.sharding import PartitionSpec as P

MESH = pl.DeviceIdType.MESH
FAR = (4, 3, 5, 2, 6, 1, 7)
F32, BF16 = jnp.float32, jnp.bfloat16
OWN = (((0, 2),), ((0, 1), (1, 2)))
NEXT = (((0, 0), (1, 1)), ((1, 0),))


def layer_kernel(
    lat_hbm, w_hbm, gain_hbm, tgt_hbm, feat, fin,
    win, w, tgt, gain_ref, own, nxt, halo, conv_in, conv_edge, zin_out, zin, zed_out, zed,
    sums, gpay, grs, crs, ya, za, yb, zb, load_sem, side_send, side_recv, z_send, z_recv, send_sem, recv_sem,
):
    tm = lax.axis_index("tm")
    row = lax.axis_index("row")
    y, zl = tm // 4, tm % 4
    x, zh, core = row // 4, (row // 2) % 2, row % 2

    def a_peer(j):
        return tm, (j // 2) * 4 + zh * 2 + j % 2

    def y_peer(j):
        return j * 4 + zl, row

    def z_peer(j):
        return y * 4 + j % 4, x * 4 + (j // 4) * 2 + core

    a_me, y_me, z_me = x * 2 + core, y, zh * 4 + zl
    has_prev, has_next, has_up, has_down = tm > 0, tm < 31, row > 0, row < 15

    barrier = pltpu.get_barrier_semaphore()
    near = ((has_prev, (tm - 1, row)), (has_next, (tm + 1, row)), (has_up, (tm, row - 1)), (has_down, (tm, row + 1)))
    expected = jnp.int32(21)
    for there, device in near:
        @pl.when(there)
        def _():
            pl.semaphore_signal(barrier, inc=1, device_id=device, device_id_type=MESH)
        expected = expected + there.astype(jnp.int32)
    for me, peer in ((a_me, a_peer), (y_me, y_peer), (z_me, z_peer)):
        for k in range(1, 8):
            pl.semaphore_signal(barrier, inc=1, device_id=peer((me + k) % 8), device_id_type=MESH)

    loads = [pltpu.make_async_copy(lat_hbm, win.at[:, 1:7], load_sem.at[0])]
    loads += [pltpu.make_async_copy(w_hbm.at[dt], w.at[dt], load_sem.at[1 + dt]) for dt in range(3)]
    loads += [pltpu.make_async_copy(tgt_hbm, tgt, load_sem.at[4])]
    loads += [pltpu.make_async_copy(gain_hbm, gain_ref, load_sem.at[5])]
    for i in (0, 3, 2, 1, 4, 5):
        loads[i].start()
    blank = jnp.zeros((2, 80, 256), BF16)
    win[:, 0] = blank
    win[:, 7] = blank

    @pl.when(row == 0)
    def _():
        halo[0] = blank

    @pl.when(row == 15)
    def _():
        halo[1] = blank

    @pl.when(tm == 0)
    def _():
        zin[...] = jnp.zeros(zin.shape, BF16)
        zed[...] = jnp.zeros(zed.shape, BF16)

    def taps(dst, o, pairs):
        @pl.loop(0, 3)
        def _(dw):
            cols = pl.ds(pl.multiple_of(dw * 256, 256), 256)
            acc = None
            for frame, dt in pairs:
                for dh in range(3):
                    piece = win[frame, dh : dh + 6].reshape(480, 256)
                    prod = jnp.dot(piece, w[dt, dh, cols], preferred_element_type=F32)
                    acc = prod if acc is None else acc + prod
            dst[o, dw] = acc

    def joined(src, o, rows, size):
        col = lax.broadcasted_iota(jnp.int32, (size, 1), 0) % 80
        left = jnp.where(col == 0, 0.0, pltpu.roll(src[o, 0, rows], 1, 0))
        right = jnp.where(col == 79, 0.0, pltpu.roll(src[o, 2, rows], size - 1, 0))
        return src[o, 1, rows] + left + right

    loads[0].wait()
    pl.semaphore_wait(barrier, expected)

    def side_copy(to):
        return pltpu.make_async_remote_copy(
            src_ref=win.at[:, 6 - 5 * to], dst_ref=halo.at[to], send_sem=side_send.at[to], recv_sem=side_recv.at[to],
            device_id=(tm, row + 1 - 2 * to), device_id_type=MESH,
        )

    def inner_copy(f):
        return pltpu.make_async_remote_copy(
            src_ref=zin_out.at[f], dst_ref=zin.at[f], send_sem=z_send.at[f], recv_sem=z_recv.at[f],
            device_id=(tm + 1, row), device_id_type=MESH,
        )

    def edge_copy(side):
        return pltpu.make_async_remote_copy(
            src_ref=zed_out.at[side], dst_ref=zed.at[side], send_sem=z_send.at[2 + side], recv_sem=z_recv.at[2 + side],
            device_id=(tm + 1, row), device_id_type=MESH,
        )

    @pl.when(has_down)
    def _():
        side_copy(0).start()

    @pl.when(has_up)
    def _():
        side_copy(1).start()

    for f in range(2):
        loads[3 - f].wait()
        taps(own, f, OWN[f])
        conv_in[f] = joined(own, f, pl.ds(80, 320), 320)
    loads[1].wait()
    for f in (1, 0):
        taps(nxt, f, NEXT[f])
        zin_out[f] = joined(nxt, f, pl.ds(80, 320), 320).astype(BF16).reshape(4, 80, 256)

        @pl.when(has_next)
        def _():
            inner_copy(f).start()

    def edge_rows(side):
        return pl.ds(pl.multiple_of(side * 400, 80), 80)

    def edge_next(side):
        other = row + 2 * side - 1

        @pl.when((other >= 0) & (other <= 15))
        def _():
            side_copy(side).wait_recv()

        dh = 2 * side
        rows = edge_rows(side)

        @pl.loop(0, 3)
        def _(dw):
            cols = pl.ds(pl.multiple_of(dw * 256, 256), 256)
            both = halo[side].reshape(160, 256)
            p0 = jnp.dot(both, w[0, dh, cols], preferred_element_type=F32)
            p1 = jnp.dot(both[80:160], w[1, dh, cols], preferred_element_type=F32)
            nxt[0, dw, rows] += p0[0:80] + p1
            nxt[1, dw, rows] += p0[80:160]

        for f in range(2):
            zed_out[side, f] = joined(nxt, f, rows, 80).astype(BF16)

        @pl.when(has_next)
        def _():
            edge_copy(side).start()

    near_side, far_side = 1 - core, core
    edge_next(near_side)

    edge_next(far_side)

    def edge_own(side, carry):
        dh = 2 * side
        rows = edge_rows(side)

        @pl.loop(0, 3)
        def _(dw):
            cols = pl.ds(pl.multiple_of(dw * 256, 256), 256)
            both = halo[side].reshape(160, 256)
            p0 = jnp.dot(both, w[2, dh, cols], preferred_element_type=F32)
            p1 = jnp.dot(both[0:80], w[1, dh, cols], preferred_element_type=F32)
            own[0, dw, rows] += p0[0:80]
            own[1, dw, rows] += p0[80:160] + p1

        for f in range(2):
            conv_edge[side, f] = joined(own, f, rows, 80)
        return carry

    lax.fori_loop(0, 2, edge_own, 0)
    loads[4].wait()
    loads[5].wait()

    def finish(conv, base, target, first):
        size = conv.shape[0]
        mean = jnp.mean(conv * conv, axis=1, keepdims=True)
        v = conv * lax.rsqrt(mean + 1e-06) * gain_ref[...][None, :]
        out = (base.reshape(size, 256).astype(F32) + v / (1.0 + jnp.exp(-v))).astype(BF16)
        dims = (((0,), (0,)), ((), ()))
        g = lax.dot_general(out, out, dims, preferred_element_type=F32)
        c = lax.dot_general(out, target.reshape(size, 128), dims, preferred_element_type=F32)
        blocks = (g[0:128, 0:128], g[0:128, 128:256], g[128:256, 128:256], c[0:128], c[128:256])
        for i, block in enumerate(blocks):
            place = slice(128 * i, 128 * i + 128)
            sums[place] = block if first else sums[place] + block
        return out

    for f in (1, 0):
        @pl.when(has_prev)
        def _():
            inner_copy(f).wait_recv()

        conv = conv_in[f] + zin[f].reshape(320, 256).astype(F32)
        feat[f, 1:5] = finish(conv, win[f, 2:6], tgt[f, 1:5], f == 1).reshape(4, 80, 256)
    for side in (near_side, far_side):
        @pl.when(has_prev)
        def _():
            edge_copy(side).wait_recv()

        conv = (conv_edge[side] + zed[side].astype(F32)).reshape(160, 256)
        out = finish(conv, win[:, 1 + 5 * side], tgt[:, 5 * side], False)
        feat[:, 5 * side] = out.reshape(2, 80, 256)

    def copy(stage, me, peer, k, src, dst):
        j = (me + k) % 8
        return pltpu.make_async_remote_copy(
            src_ref=src(j), dst_ref=dst(me), send_sem=send_sem.at[stage, j], recv_sem=recv_sem.at[stage, me],
            device_id=peer(j), device_id_type=MESH,
        )

    def arrival(stage, me, peer, k, src, dst):
        j = (me + k) % 8
        return pltpu.make_async_remote_copy(
            src_ref=src(j), dst_ref=dst(j), send_sem=send_sem.at[stage, j], recv_sem=recv_sem.at[stage, j],
            device_id=peer(j), device_id_type=MESH,
        )

    def send(stage, me, peer, src, dst):
        for k in FAR:
            copy(stage, me, peer, k, src, dst).start()

    def receive(stage, me, peer, src, dst):
        for k in FAR:
            arrival(stage, me, peer, k, src, dst).wait_recv()

    def drain(stage, me, peer, src, dst):
        for k in FAR:
            copy(stage, me, peer, k, src, dst).wait_send()

    def chunk(ref, size):
        return lambda j: ref.at[pl.ds(pl.multiple_of(j * size, 8), size)]

    def slot(ref):
        return lambda j: ref.at[j]

    def total(ref):
        acc = ref[0].astype(F32)
        for j in range(1, 8):
            acc = acc + ref[j].astype(F32)
        return acc

    gpay[...] = sums[0:384].astype(BF16)
    gplace = pl.ds(pl.multiple_of(a_me * 48, 16), 48)
    cplace = pl.ds(pl.multiple_of(384 + a_me * 32, 8), 32)
    s0 = (0, a_me, a_peer, chunk(gpay, 48), slot(grs))
    s1 = (1, a_me, a_peer, lambda j: sums.at[pl.ds(pl.multiple_of(384 + j * 32, 8), 32)], slot(crs))
    send(*s0)
    send(*s1)
    grs[a_me] = gpay[gplace]
    crs[a_me] = sums[cplace]
    receive(*s0)
    ya[y_me] = total(grs).astype(BF16)
    s2 = (2, y_me, y_peer, lambda j: ya.at[y_me], slot(ya))
    send(*s2)
    receive(*s1)
    za[z_me] = total(crs)
    s3 = (3, z_me, z_peer, lambda j: za.at[z_me], slot(za))
    send(*s3)
    receive(*s2)
    zb[z_me] = total(ya).astype(BF16)
    s4 = (4, z_me, z_peer, lambda j: zb.at[z_me], slot(zb))
    send(*s4)
    receive(*s3)
    yb[y_me] = total(za)
    s5 = (5, y_me, y_peer, lambda j: yb.at[y_me], slot(yb))
    send(*s5)
    receive(*s4)
    fin[pl.ds(pl.multiple_of(a_me * 48, 16), 48)] = total(zb)
    s6 = (6, a_me, a_peer, lambda j: fin.at[gplace], chunk(fin, 48))
    send(*s6)
    receive(*s5)
    fin[cplace] = total(yb)
    s7 = (7, a_me, a_peer, lambda j: fin.at[cplace], lambda j: fin.at[pl.ds(pl.multiple_of(384 + j * 32, 8), 32)])
    send(*s7)
    receive(*s6)
    receive(*s7)

    for s in (s0, s1, s2, s3, s4, s5, s6, s7):
        drain(*s)

    @pl.when(has_down)
    def _():
        side_copy(0).wait_send()

    @pl.when(has_up)
    def _():
        side_copy(1).wait_send()

    @pl.when(has_next)
    def _():
        for i in range(2):
            inner_copy(i).wait_send()
            edge_copy(i).wait_send()


def write_kernel(scale, feat, fin, feat_out, gram_out, cross_out, gram, cross, sem):
    first = pltpu.make_async_copy(feat, feat_out, sem.at[0])
    first.start()
    cross[...] = fin[384:640] * scale
    second = pltpu.make_async_copy(cross, cross_out, sem.at[1])
    second.start()
    gram[0:128, 0:128] = fin[0:128] * scale
    gram[0:128, 128:256] = fin[128:256] * scale
    gram[128:256, 0:128] = fin[128:256].T * scale
    gram[128:256, 128:256] = fin[256:384] * scale
    third = pltpu.make_async_copy(gram, gram_out, sem.at[2])
    third.start()
    first.wait()
    second.wait()
    third.wait()


def on_device(latents, conv_weight, norm_gain, depth_target):
    vmem = pl.BlockSpec(memory_space=pltpu.VMEM)
    anywhere = pl.BlockSpec(memory_space=pltpu.HBM)
    dma = pltpu.SemaphoreType.DMA
    feat, fin = pl.pallas_call(
        layer_kernel,
        out_shape=(jax.ShapeDtypeStruct((2, 6, 80, 256), BF16), jax.ShapeDtypeStruct((640, 128), F32)),
        in_specs=[anywhere, anywhere, anywhere, anywhere],
        out_specs=(vmem, vmem),
        scratch_shapes=[
            pltpu.VMEM((2, 8, 80, 256), BF16),
            pltpu.VMEM((3, 3, 768, 256), BF16),
            pltpu.VMEM((2, 6, 80, 128), BF16),
            pltpu.VMEM((256,), F32),
            pltpu.VMEM((2, 3, 480, 256), F32),
            pltpu.VMEM((2, 3, 480, 256), F32),
            pltpu.VMEM((2, 2, 80, 256), BF16),
            pltpu.VMEM((2, 320, 256), F32),
            pltpu.VMEM((2, 2, 80, 256), F32),
            pltpu.VMEM((2, 4, 80, 256), BF16),
            pltpu.VMEM((2, 4, 80, 256), BF16),
            pltpu.VMEM((2, 2, 80, 256), BF16),
            pltpu.VMEM((2, 2, 80, 256), BF16),
            pltpu.VMEM((640, 128), F32),
            pltpu.VMEM((384, 128), BF16),
            pltpu.VMEM((8, 48, 128), BF16),
            pltpu.VMEM((8, 32, 128), F32),
            pltpu.VMEM((8, 48, 128), BF16),
            pltpu.VMEM((8, 32, 128), F32),
            pltpu.VMEM((8, 32, 128), F32),
            pltpu.VMEM((8, 48, 128), BF16),
            dma((6,)),
            dma((2,)),
            dma((2,)),
            dma((4,)),
            dma((4,)),
            dma((8, 8)),
            dma((8, 8)),
        ],
        compiler_params=pltpu.CompilerParams(collective_id=0, has_side_effects=True, vmem_limit_bytes=40 << 20),
    )(*(pltpu.with_memory_space_constraint(a, pltpu.HBM) for a in (latents, conv_weight, norm_gain, depth_target)))
    count = 960 * lax.axis_size("tm") * lax.axis_size("row")
    return pl.pallas_call(
        functools.partial(write_kernel, 1.0 / count),
        out_shape=(
            jax.ShapeDtypeStruct((2, 6, 80, 256), BF16),
            jax.ShapeDtypeStruct((256, 256), F32),
            jax.ShapeDtypeStruct((256, 128), F32),
        ),
        in_specs=[vmem, vmem],
        out_specs=(anywhere, anywhere, anywhere),
        scratch_shapes=[pltpu.VMEM((256, 256), F32), pltpu.VMEM((256, 128), F32), dma((3,))],
        compiler_params=pltpu.CompilerParams(vmem_limit_bytes=40 << 20),
    )(feat, fin)


def solution(mesh):
    in_specs = (P("tm", "row", None, None), P(), P(), P("tm", "row", None, None))
    out_specs = (P("tm", "row", None, None), P(), P())
    return jax.shard_map(
        on_device, mesh=mesh, in_specs=in_specs, out_specs=out_specs, check_vma=False
    )
```

```python
import functools

import jax
import jax.numpy as jnp
from jax import lax
from jax.experimental import pallas as pl
from jax.experimental.pallas import tpu as pltpu
from jax.sharding import PartitionSpec as P

MESH = pl.DeviceIdType.MESH
FAR = (4, 3, 5, 2, 6, 1, 7)
F32, BF16 = jnp.float32, jnp.bfloat16
OWN = (((0, 2),), ((0, 1), (1, 2)))
NEXT = (((0, 0), (1, 1)), ((1, 0),))


def layer_kernel(
    lat_hbm, w_hbm, gain_hbm, tgt_hbm, feat, fin,
    win, w, tgt, gain_ref, own, nxt, halo, conv_in, conv_edge, zin_out, zin, zed_out, zed,
    sums, gpay, grs, crs, ya, za, yb, zb, load_sem, side_send, side_recv, z_send, z_recv, send_sem, recv_sem,
):
    tm = lax.axis_index("tm")
    row = lax.axis_index("row")
    y, zl = tm // 4, tm % 4
    x, zh, core = row // 4, (row // 2) % 2, row % 2

    def a_peer(j):
        return tm, (j // 2) * 4 + zh * 2 + j % 2

    def y_peer(j):
        return j * 4 + zl, row

    def z_peer(j):
        return y * 4 + j % 4, x * 4 + (j // 4) * 2 + core

    a_me, y_me, z_me = x * 2 + core, y, zh * 4 + zl
    has_prev, has_next, has_up, has_down = tm > 0, tm < 31, row > 0, row < 15

    barrier = pltpu.get_barrier_semaphore()
    near = ((has_prev, (tm - 1, row)), (has_next, (tm + 1, row)), (has_up, (tm, row - 1)), (has_down, (tm, row + 1)))
    for k in FAR:
        for me, peer in ((z_me, z_peer), (y_me, y_peer), (a_me, a_peer)):
            pl.semaphore_signal(barrier, inc=1, device_id=peer((me + k) % 8), device_id_type=MESH)
    expected = jnp.int32(21)
    for there, device in near:
        @pl.when(there)
        def _():
            pl.semaphore_signal(barrier, inc=1, device_id=device, device_id_type=MESH)
        expected = expected + there.astype(jnp.int32)

    loads = [pltpu.make_async_copy(lat_hbm, win.at[:, 1:7], load_sem.at[0])]
    loads += [pltpu.make_async_copy(w_hbm.at[dt], w.at[dt], load_sem.at[1 + dt]) for dt in range(3)]
    loads += [pltpu.make_async_copy(tgt_hbm, tgt, load_sem.at[4])]
    loads += [pltpu.make_async_copy(gain_hbm, gain_ref, load_sem.at[5])]
    for i in (0, 3, 2, 1, 4, 5):
        loads[i].start()
    blank = jnp.zeros((2, 80, 256), BF16)
    win[:, 0] = blank
    win[:, 7] = blank

    @pl.when(row == 0)
    def _():
        halo[0] = blank

    @pl.when(row == 15)
    def _():
        halo[1] = blank

    @pl.when(tm == 0)
    def _():
        zin[...] = jnp.zeros(zin.shape, BF16)
        zed[...] = jnp.zeros(zed.shape, BF16)

    def taps(dst, o, pairs):
        @pl.loop(0, 3)
        def _(dw):
            cols = pl.ds(pl.multiple_of(dw * 256, 256), 256)
            acc = None
            for frame, dt in pairs:
                for dh in range(3):
                    piece = win[frame, dh : dh + 6].reshape(480, 256)
                    prod = jnp.dot(piece, w[dt, dh, cols], preferred_element_type=F32)
                    acc = prod if acc is None else acc + prod
            dst[o, dw] = acc

    def joined(src, o, rows, size):
        col = lax.broadcasted_iota(jnp.int32, (size, 1), 0) % 80
        left = jnp.where(col == 0, 0.0, pltpu.roll(src[o, 0, rows], 1, 0))
        right = jnp.where(col == 79, 0.0, pltpu.roll(src[o, 2, rows], size - 1, 0))
        return src[o, 1, rows] + left + right

    loads[0].wait()
    pl.semaphore_wait(barrier, expected)

    def side_copy(to):
        return pltpu.make_async_remote_copy(
            src_ref=win.at[:, 6 - 5 * to], dst_ref=halo.at[to], send_sem=side_send.at[to], recv_sem=side_recv.at[to],
            device_id=(tm, row + 1 - 2 * to), device_id_type=MESH,
        )

    def inner_copy(f):
        return pltpu.make_async_remote_copy(
            src_ref=zin_out.at[f], dst_ref=zin.at[f], send_sem=z_send.at[f], recv_sem=z_recv.at[f],
            device_id=(tm + 1, row), device_id_type=MESH,
        )

    def edge_copy(side):
        return pltpu.make_async_remote_copy(
            src_ref=zed_out.at[side], dst_ref=zed.at[side], send_sem=z_send.at[2 + side], recv_sem=z_recv.at[2 + side],
            device_id=(tm + 1, row), device_id_type=MESH,
        )

    @pl.when(has_down)
    def _():
        side_copy(0).start()

    @pl.when(has_up)
    def _():
        side_copy(1).start()

    for i in (1, 2, 3):
        loads[i].wait()

    def own_part():
        for f in range(2):
            taps(own, f, OWN[f])
            conv_in[f] = joined(own, f, pl.ds(80, 320), 320)

    @pl.when(zl == 3)
    def _():
        own_part()

    for f in (1, 0):
        taps(nxt, f, NEXT[f])
        zin_out[f] = joined(nxt, f, pl.ds(80, 320), 320).astype(BF16).reshape(4, 80, 256)

        @pl.when(has_next)
        def _():
            inner_copy(f).start()

    def edge_rows(side):
        return pl.ds(pl.multiple_of(side * 400, 80), 80)

    def edge_next(side):
        other = row + 2 * side - 1

        @pl.when((other >= 0) & (other <= 15))
        def _():
            side_copy(side).wait_recv()

        dh = 2 * side
        rows = edge_rows(side)

        @pl.loop(0, 3)
        def _(dw):
            cols = pl.ds(pl.multiple_of(dw * 256, 256), 256)
            both = halo[side].reshape(160, 256)
            p0 = jnp.dot(both, w[0, dh, cols], preferred_element_type=F32)
            p1 = jnp.dot(both[80:160], w[1, dh, cols], preferred_element_type=F32)
            nxt[0, dw, rows] += p0[0:80] + p1
            nxt[1, dw, rows] += p0[80:160]

        for f in range(2):
            zed_out[side, f] = joined(nxt, f, rows, 80).astype(BF16)

        @pl.when(has_next)
        def _():
            edge_copy(side).start()

    near_side, far_side = 1 - core, core
    edge_next(near_side)

    edge_next(far_side)

    @pl.when(zl != 3)
    def _():
        own_part()

    def edge_own(side, carry):
        dh = 2 * side
        rows = edge_rows(side)

        @pl.loop(0, 3)
        def _(dw):
            cols = pl.ds(pl.multiple_of(dw * 256, 256), 256)
            both = halo[side].reshape(160, 256)
            p0 = jnp.dot(both, w[2, dh, cols], preferred_element_type=F32)
            p1 = jnp.dot(both[0:80], w[1, dh, cols], preferred_element_type=F32)
            own[0, dw, rows] += p0[0:80]
            own[1, dw, rows] += p0[80:160] + p1

        for f in range(2):
            conv_edge[side, f] = joined(own, f, rows, 80)
        return carry

    lax.fori_loop(0, 2, edge_own, 0)
    loads[4].wait()
    loads[5].wait()

    def finish(conv, base, target, first):
        size = conv.shape[0]
        mean = jnp.mean(conv * conv, axis=1, keepdims=True)
        v = conv * lax.rsqrt(mean + 1e-06) * gain_ref[...][None, :]
        out = (base.reshape(size, 256).astype(F32) + v / (1.0 + jnp.exp(-v))).astype(BF16)
        dims = (((0,), (0,)), ((), ()))
        g = lax.dot_general(out, out, dims, preferred_element_type=F32)
        c = lax.dot_general(out, target.reshape(size, 128), dims, preferred_element_type=F32)
        blocks = (g[0:128, 0:128], g[0:128, 128:256], g[128:256, 128:256], c[0:128], c[128:256])
        for i, block in enumerate(blocks):
            place = slice(128 * i, 128 * i + 128)
            sums[place] = block if first else sums[place] + block
        return out

    for f in (1, 0):
        @pl.when(has_prev)
        def _():
            inner_copy(f).wait_recv()

        conv = conv_in[f] + zin[f].reshape(320, 256).astype(F32)
        feat[f, 1:5] = finish(conv, win[f, 2:6], tgt[f, 1:5], f == 1).reshape(4, 80, 256)
    for side in (near_side, far_side):
        @pl.when(has_prev)
        def _():
            edge_copy(side).wait_recv()

        conv = (conv_edge[side] + zed[side].astype(F32)).reshape(160, 256)
        out = finish(conv, win[:, 1 + 5 * side], tgt[:, 5 * side], False)
        feat[:, 5 * side] = out.reshape(2, 80, 256)

    def copy(stage, me, peer, k, src, dst):
        j = (me + k) % 8
        return pltpu.make_async_remote_copy(
            src_ref=src(j), dst_ref=dst(me), send_sem=send_sem.at[stage, j], recv_sem=recv_sem.at[stage, me],
            device_id=peer(j), device_id_type=MESH,
        )

    def arrival(stage, me, peer, k, src, dst):
        j = (me + k) % 8
        return pltpu.make_async_remote_copy(
            src_ref=src(j), dst_ref=dst(j), send_sem=send_sem.at[stage, j], recv_sem=recv_sem.at[stage, j],
            device_id=peer(j), device_id_type=MESH,
        )

    def send(stage, me, peer, src, dst):
        for k in FAR:
            copy(stage, me, peer, k, src, dst).start()

    def receive(stage, me, peer, src, dst):
        for k in FAR:
            arrival(stage, me, peer, k, src, dst).wait_recv()

    def drain(stage, me, peer, src, dst):
        for k in FAR:
            copy(stage, me, peer, k, src, dst).wait_send()

    def chunk(ref, size):
        return lambda j: ref.at[pl.ds(pl.multiple_of(j * size, 8), size)]

    def slot(ref):
        return lambda j: ref.at[j]

    def total(ref):
        acc = ref[0].astype(F32)
        for j in range(1, 8):
            acc = acc + ref[j].astype(F32)
        return acc

    gpay[...] = sums[0:384].astype(BF16)
    gplace = pl.ds(pl.multiple_of(a_me * 48, 16), 48)
    cplace = pl.ds(pl.multiple_of(384 + a_me * 32, 8), 32)
    s0 = (0, a_me, a_peer, chunk(gpay, 48), slot(grs))
    s1 = (1, a_me, a_peer, lambda j: sums.at[pl.ds(pl.multiple_of(384 + j * 32, 8), 32)], slot(crs))
    send(*s0)
    send(*s1)
    grs[a_me] = gpay[gplace]
    crs[a_me] = sums[cplace]
    receive(*s0)
    ya[y_me] = total(grs).astype(BF16)
    s2 = (2, y_me, y_peer, lambda j: ya.at[y_me], slot(ya))
    send(*s2)
    receive(*s1)
    za[z_me] = total(crs)
    s3 = (3, z_me, z_peer, lambda j: za.at[z_me], slot(za))
    send(*s3)
    receive(*s2)
    zb[z_me] = total(ya).astype(BF16)
    s4 = (4, z_me, z_peer, lambda j: zb.at[z_me], slot(zb))
    send(*s4)
    receive(*s3)
    yb[y_me] = total(za)
    s5 = (5, y_me, y_peer, lambda j: yb.at[y_me], slot(yb))
    send(*s5)
    receive(*s4)
    fin[pl.ds(pl.multiple_of(a_me * 48, 16), 48)] = total(zb)
    s6 = (6, a_me, a_peer, lambda j: fin.at[gplace], chunk(fin, 48))
    send(*s6)
    receive(*s5)
    fin[cplace] = total(yb)
    s7 = (7, a_me, a_peer, lambda j: fin.at[cplace], lambda j: fin.at[pl.ds(pl.multiple_of(384 + j * 32, 8), 32)])
    send(*s7)
    receive(*s6)
    receive(*s7)

    for s in (s0, s1, s2, s3, s4, s5, s6, s7):
        drain(*s)

    @pl.when(has_down)
    def _():
        side_copy(0).wait_send()

    @pl.when(has_up)
    def _():
        side_copy(1).wait_send()

    @pl.when(has_next)
    def _():
        for i in range(2):
            inner_copy(i).wait_send()
            edge_copy(i).wait_send()


def write_kernel(scale, feat, fin, feat_out, gram_out, cross_out, gram, cross, sem):
    first = pltpu.make_async_copy(feat, feat_out, sem.at[0])
    first.start()
    cross[...] = fin[384:640] * scale
    second = pltpu.make_async_copy(cross, cross_out, sem.at[1])
    second.start()
    gram[0:128, 0:128] = fin[0:128] * scale
    gram[0:128, 128:256] = fin[128:256] * scale
    gram[128:256, 0:128] = fin[128:256].T * scale
    gram[128:256, 128:256] = fin[256:384] * scale
    third = pltpu.make_async_copy(gram, gram_out, sem.at[2])
    third.start()
    first.wait()
    second.wait()
    third.wait()


def on_device(latents, conv_weight, norm_gain, depth_target):
    vmem = pl.BlockSpec(memory_space=pltpu.VMEM)
    anywhere = pl.BlockSpec(memory_space=pltpu.HBM)
    dma = pltpu.SemaphoreType.DMA
    feat, fin = pl.pallas_call(
        layer_kernel,
        out_shape=(jax.ShapeDtypeStruct((2, 6, 80, 256), BF16), jax.ShapeDtypeStruct((640, 128), F32)),
        in_specs=[anywhere, anywhere, anywhere, anywhere],
        out_specs=(vmem, vmem),
        scratch_shapes=[
            pltpu.VMEM((2, 8, 80, 256), BF16),
            pltpu.VMEM((3, 3, 768, 256), BF16),
            pltpu.VMEM((2, 6, 80, 128), BF16),
            pltpu.VMEM((256,), F32),
            pltpu.VMEM((2, 3, 480, 256), F32),
            pltpu.VMEM((2, 3, 480, 256), F32),
            pltpu.VMEM((2, 2, 80, 256), BF16),
            pltpu.VMEM((2, 320, 256), F32),
            pltpu.VMEM((2, 2, 80, 256), F32),
            pltpu.VMEM((2, 4, 80, 256), BF16),
            pltpu.VMEM((2, 4, 80, 256), BF16),
            pltpu.VMEM((2, 2, 80, 256), BF16),
            pltpu.VMEM((2, 2, 80, 256), BF16),
            pltpu.VMEM((640, 128), F32),
            pltpu.VMEM((384, 128), BF16),
            pltpu.VMEM((8, 48, 128), BF16),
            pltpu.VMEM((8, 32, 128), F32),
            pltpu.VMEM((8, 48, 128), BF16),
            pltpu.VMEM((8, 32, 128), F32),
            pltpu.VMEM((8, 32, 128), F32),
            pltpu.VMEM((8, 48, 128), BF16),
            dma((6,)),
            dma((2,)),
            dma((2,)),
            dma((4,)),
            dma((4,)),
            dma((8, 8)),
            dma((8, 8)),
        ],
        compiler_params=pltpu.CompilerParams(collective_id=0, has_side_effects=True, vmem_limit_bytes=40 << 20),
    )(*(pltpu.with_memory_space_constraint(a, pltpu.HBM) for a in (latents, conv_weight, norm_gain, depth_target)))
    count = 960 * lax.axis_size("tm") * lax.axis_size("row")
    return pl.pallas_call(
        functools.partial(write_kernel, 1.0 / count),
        out_shape=(
            jax.ShapeDtypeStruct((2, 6, 80, 256), BF16),
            jax.ShapeDtypeStruct((256, 256), F32),
            jax.ShapeDtypeStruct((256, 128), F32),
        ),
        in_specs=[vmem, vmem],
        out_specs=(anywhere, anywhere, anywhere),
        scratch_shapes=[pltpu.VMEM((256, 256), F32), pltpu.VMEM((256, 128), F32), dma((3,))],
        compiler_params=pltpu.CompilerParams(vmem_limit_bytes=40 << 20),
    )(feat, fin)


def solution(mesh):
    in_specs = (P("tm", "row", None, None), P(), P(), P("tm", "row", None, None))
    out_specs = (P("tm", "row", None, None), P(), P())
    return jax.shard_map(
        on_device, mesh=mesh, in_specs=in_specs, out_specs=out_specs, check_vma=False
    )
```

```python
import functools

import jax
import jax.numpy as jnp
from jax import lax
from jax.experimental import pallas as pl
from jax.experimental.pallas import tpu as pltpu
from jax.sharding import PartitionSpec as P

MESH = pl.DeviceIdType.MESH
FAR = (4, 3, 5, 2, 6, 1, 7)
F32, BF16 = jnp.float32, jnp.bfloat16
OWN = (((0, 2),), ((0, 1), (1, 2)))
NEXT = (((0, 0), (1, 1)), ((1, 0),))


def layer_kernel(
    lat_hbm, w_hbm, gain_hbm, tgt_hbm, feat, fin,
    win, w, tgt, gain_ref, own, nxt, halo, conv_in, conv_edge, zin_out, zin, zed_out, zed,
    sums, gpay, grs, crs, ya, za, yb, zb, load_sem, side_send, side_recv, z_send, z_recv, send_sem, recv_sem,
):
    tm = lax.axis_index("tm")
    row = lax.axis_index("row")
    y, zl = tm // 4, tm % 4
    x, zh, core = row // 4, (row // 2) % 2, row % 2

    def a_peer(j):
        return tm, (j // 2) * 4 + zh * 2 + j % 2

    def y_peer(j):
        return j * 4 + zl, row

    def z_peer(j):
        return y * 4 + j % 4, x * 4 + (j // 4) * 2 + core

    a_me, y_me, z_me = x * 2 + core, y, zh * 4 + zl
    has_prev, has_next, has_up, has_down = tm > 0, tm < 31, row > 0, row < 15

    barrier = pltpu.get_barrier_semaphore()
    near = ((has_prev, (tm - 1, row)), (has_next, (tm + 1, row)), (has_up, (tm, row - 1)), (has_down, (tm, row + 1)))
    expected = jnp.int32(21)
    for there, device in near:
        @pl.when(there)
        def _():
            pl.semaphore_signal(barrier, inc=1, device_id=device, device_id_type=MESH)
        expected = expected + there.astype(jnp.int32)
    for me, peer in ((a_me, a_peer), (y_me, y_peer), (z_me, z_peer)):
        for k in range(1, 8):
            pl.semaphore_signal(barrier, inc=1, device_id=peer((me + k) % 8), device_id_type=MESH)

    loads = [pltpu.make_async_copy(lat_hbm, win.at[:, 1:7], load_sem.at[0])]
    loads += [pltpu.make_async_copy(w_hbm.at[dt], w.at[dt], load_sem.at[1 + dt]) for dt in range(3)]
    loads += [pltpu.make_async_copy(tgt_hbm, tgt, load_sem.at[4])]
    loads += [pltpu.make_async_copy(gain_hbm, gain_ref, load_sem.at[5])]
    for i in (0, 3, 2, 1, 4, 5):
        loads[i].start()
    blank = jnp.zeros((2, 80, 256), BF16)
    win[:, 0] = blank
    win[:, 7] = blank

    @pl.when(row == 0)
    def _():
        halo[0] = blank

    @pl.when(row == 15)
    def _():
        halo[1] = blank

    @pl.when(tm == 0)
    def _():
        zin[...] = jnp.zeros(zin.shape, BF16)
        zed[...] = jnp.zeros(zed.shape, BF16)

    def taps(dst, o, pairs):
        @pl.loop(0, 3)
        def _(dw):
            cols = pl.ds(pl.multiple_of(dw * 256, 256), 256)
            acc = None
            for frame, dt in pairs:
                for dh in range(3):
                    piece = win[frame, dh : dh + 6].reshape(480, 256)
                    prod = jnp.dot(piece, w[dt, dh, cols], preferred_element_type=F32)
                    acc = prod if acc is None else acc + prod
            dst[o, dw] = acc

    def joined(src, o, rows, size):
        col = lax.broadcasted_iota(jnp.int32, (size, 1), 0) % 80
        left = jnp.where(col == 0, 0.0, pltpu.roll(src[o, 0, rows], 1, 0))
        right = jnp.where(col == 79, 0.0, pltpu.roll(src[o, 2, rows], size - 1, 0))
        return src[o, 1, rows] + left + right

    loads[0].wait()
    pl.semaphore_wait(barrier, expected)

    def side_copy(to):
        return pltpu.make_async_remote_copy(
            src_ref=win.at[:, 6 - 5 * to], dst_ref=halo.at[to], send_sem=side_send.at[to], recv_sem=side_recv.at[to],
            device_id=(tm, row + 1 - 2 * to), device_id_type=MESH,
        )

    def inner_copy(f):
        return pltpu.make_async_remote_copy(
            src_ref=zin_out.at[f], dst_ref=zin.at[f], send_sem=z_send.at[f], recv_sem=z_recv.at[f],
            device_id=(tm + 1, row), device_id_type=MESH,
        )

    def edge_copy(side):
        return pltpu.make_async_remote_copy(
            src_ref=zed_out.at[side], dst_ref=zed.at[side], send_sem=z_send.at[2 + side], recv_sem=z_recv.at[2 + side],
            device_id=(tm + 1, row), device_id_type=MESH,
        )

    @pl.when(has_down)
    def _():
        side_copy(0).start()

    @pl.when(has_up)
    def _():
        side_copy(1).start()

    for f in range(2):
        loads[3 - f].wait()
        taps(own, f, OWN[f])
        conv_in[f] = joined(own, f, pl.ds(80, 320), 320)
    loads[1].wait()
    for f in (1, 0):
        taps(nxt, f, NEXT[f])
        zin_out[f] = joined(nxt, f, pl.ds(80, 320), 320).astype(BF16).reshape(4, 80, 256)

        @pl.when(has_next)
        def _():
            inner_copy(f).start()

    def edge_rows(side):
        return pl.ds(pl.multiple_of(side * 400, 80), 80)

    def edge_next(side):
        other = row + 2 * side - 1

        @pl.when((other >= 0) & (other <= 15))
        def _():
            side_copy(side).wait_recv()

        dh = 2 * side
        rows = edge_rows(side)

        @pl.loop(0, 3)
        def _(dw):
            cols = pl.ds(pl.multiple_of(dw * 256, 256), 256)
            both = halo[side].reshape(160, 256)
            p0 = jnp.dot(both, w[0, dh, cols], preferred_element_type=F32)
            p1 = jnp.dot(both[80:160], w[1, dh, cols], preferred_element_type=F32)
            nxt[0, dw, rows] += p0[0:80] + p1
            nxt[1, dw, rows] += p0[80:160]

        for f in range(2):
            zed_out[side, f] = joined(nxt, f, rows, 80).astype(BF16)

        @pl.when(has_next)
        def _():
            edge_copy(side).start()

    near_side, far_side = 1 - core, core
    edge_next(near_side)

    edge_next(far_side)

    def edge_own(side, carry):
        dh = 2 * side
        rows = edge_rows(side)

        @pl.loop(0, 3)
        def _(dw):
            cols = pl.ds(pl.multiple_of(dw * 256, 256), 256)
            both = halo[side].reshape(160, 256)
            p0 = jnp.dot(both, w[2, dh, cols], preferred_element_type=F32)
            p1 = jnp.dot(both[0:80], w[1, dh, cols], preferred_element_type=F32)
            own[0, dw, rows] += p0[0:80]
            own[1, dw, rows] += p0[80:160] + p1

        for f in range(2):
            conv_edge[side, f] = joined(own, f, rows, 80)
        return carry

    lax.fori_loop(0, 2, edge_own, 0)
    loads[4].wait()
    loads[5].wait()

    def copy(stage, me, peer, k, src, dst):
        j = (me + k) % 8
        return pltpu.make_async_remote_copy(
            src_ref=src(j), dst_ref=dst(me), send_sem=send_sem.at[stage, j], recv_sem=recv_sem.at[stage, me],
            device_id=peer(j), device_id_type=MESH,
        )

    def arrival(stage, me, peer, k, src, dst):
        j = (me + k) % 8
        return pltpu.make_async_remote_copy(
            src_ref=src(j), dst_ref=dst(j), send_sem=send_sem.at[stage, j], recv_sem=recv_sem.at[stage, j],
            device_id=peer(j), device_id_type=MESH,
        )

    def send(stage, me, peer, src, dst):
        for k in FAR:
            copy(stage, me, peer, k, src, dst).start()

    def receive(stage, me, peer, src, dst):
        for k in FAR:
            arrival(stage, me, peer, k, src, dst).wait_recv()

    def drain(stage, me, peer, src, dst):
        for k in FAR:
            copy(stage, me, peer, k, src, dst).wait_send()

    def chunk(ref, size):
        return lambda j: ref.at[pl.ds(pl.multiple_of(j * size, 8), size)]

    def slot(ref):
        return lambda j: ref.at[j]

    def total(ref):
        acc = ref[0].astype(F32)
        for j in range(1, 8):
            acc = acc + ref[j].astype(F32)
        return acc

    s1 = (1, a_me, a_peer, lambda j: sums.at[pl.ds(pl.multiple_of(384 + j * 32, 8), 32)], slot(crs))

    def finish(conv, base, target, first, last=False):
        size = conv.shape[0]
        mean = jnp.mean(conv * conv, axis=1, keepdims=True)
        v = conv * lax.rsqrt(mean + 1e-06) * gain_ref[...][None, :]
        out = (base.reshape(size, 256).astype(F32) + v / (1.0 + jnp.exp(-v))).astype(BF16)
        dims = (((0,), (0,)), ((), ()))
        c = lax.dot_general(out, target.reshape(size, 128), dims, preferred_element_type=F32)
        sums[384:640] = c if first else sums[384:640] + c
        if last:
            send(*s1)
        g = lax.dot_general(out, out, dims, preferred_element_type=F32)
        for i, block in enumerate((g[0:128, 0:128], g[0:128, 128:256], g[128:256, 128:256])):
            place = slice(128 * i, 128 * i + 128)
            sums[place] = block if first else sums[place] + block
        return out

    for f in (1, 0):
        @pl.when(has_prev)
        def _():
            inner_copy(f).wait_recv()

        conv = conv_in[f] + zin[f].reshape(320, 256).astype(F32)
        feat[f, 1:5] = finish(conv, win[f, 2:6], tgt[f, 1:5], f == 1).reshape(4, 80, 256)
    for last, side in ((False, near_side), (True, far_side)):
        @pl.when(has_prev)
        def _():
            edge_copy(side).wait_recv()

        conv = (conv_edge[side] + zed[side].astype(F32)).reshape(160, 256)
        out = finish(conv, win[:, 1 + 5 * side], tgt[:, 5 * side], False, last)
        feat[:, 5 * side] = out.reshape(2, 80, 256)

    gpay[...] = sums[0:384].astype(BF16)
    gplace = pl.ds(pl.multiple_of(a_me * 48, 16), 48)
    cplace = pl.ds(pl.multiple_of(384 + a_me * 32, 8), 32)
    s0 = (0, a_me, a_peer, chunk(gpay, 48), slot(grs))
    send(*s0)
    grs[a_me] = gpay[gplace]
    crs[a_me] = sums[cplace]
    receive(*s0)
    ya[y_me] = total(grs).astype(BF16)
    s2 = (2, y_me, y_peer, lambda j: ya.at[y_me], slot(ya))
    send(*s2)
    receive(*s1)
    za[z_me] = total(crs)
    s3 = (3, z_me, z_peer, lambda j: za.at[z_me], slot(za))
    send(*s3)
    receive(*s2)
    zb[z_me] = total(ya).astype(BF16)
    s4 = (4, z_me, z_peer, lambda j: zb.at[z_me], slot(zb))
    send(*s4)
    receive(*s3)
    yb[y_me] = total(za)
    s5 = (5, y_me, y_peer, lambda j: yb.at[y_me], slot(yb))
    send(*s5)
    receive(*s4)
    fin[pl.ds(pl.multiple_of(a_me * 48, 16), 48)] = total(zb)
    s6 = (6, a_me, a_peer, lambda j: fin.at[gplace], chunk(fin, 48))
    send(*s6)
    receive(*s5)
    fin[cplace] = total(yb)
    s7 = (7, a_me, a_peer, lambda j: fin.at[cplace], lambda j: fin.at[pl.ds(pl.multiple_of(384 + j * 32, 8), 32)])
    send(*s7)
    receive(*s6)
    receive(*s7)

    for s in (s0, s1, s2, s3, s4, s5, s6, s7):
        drain(*s)

    @pl.when(has_down)
    def _():
        side_copy(0).wait_send()

    @pl.when(has_up)
    def _():
        side_copy(1).wait_send()

    @pl.when(has_next)
    def _():
        for i in range(2):
            inner_copy(i).wait_send()
            edge_copy(i).wait_send()


def write_kernel(scale, feat, fin, feat_out, gram_out, cross_out, gram, cross, sem):
    first = pltpu.make_async_copy(feat, feat_out, sem.at[0])
    first.start()
    cross[...] = fin[384:640] * scale
    second = pltpu.make_async_copy(cross, cross_out, sem.at[1])
    second.start()
    gram[0:128, 0:128] = fin[0:128] * scale
    gram[0:128, 128:256] = fin[128:256] * scale
    gram[128:256, 0:128] = fin[128:256].T * scale
    gram[128:256, 128:256] = fin[256:384] * scale
    third = pltpu.make_async_copy(gram, gram_out, sem.at[2])
    third.start()
    first.wait()
    second.wait()
    third.wait()


def on_device(latents, conv_weight, norm_gain, depth_target):
    vmem = pl.BlockSpec(memory_space=pltpu.VMEM)
    anywhere = pl.BlockSpec(memory_space=pltpu.HBM)
    dma = pltpu.SemaphoreType.DMA
    feat, fin = pl.pallas_call(
        layer_kernel,
        out_shape=(jax.ShapeDtypeStruct((2, 6, 80, 256), BF16), jax.ShapeDtypeStruct((640, 128), F32)),
        in_specs=[anywhere, anywhere, anywhere, anywhere],
        out_specs=(vmem, vmem),
        scratch_shapes=[
            pltpu.VMEM((2, 8, 80, 256), BF16),
            pltpu.VMEM((3, 3, 768, 256), BF16),
            pltpu.VMEM((2, 6, 80, 128), BF16),
            pltpu.VMEM((256,), F32),
            pltpu.VMEM((2, 3, 480, 256), F32),
            pltpu.VMEM((2, 3, 480, 256), F32),
            pltpu.VMEM((2, 2, 80, 256), BF16),
            pltpu.VMEM((2, 320, 256), F32),
            pltpu.VMEM((2, 2, 80, 256), F32),
            pltpu.VMEM((2, 4, 80, 256), BF16),
            pltpu.VMEM((2, 4, 80, 256), BF16),
            pltpu.VMEM((2, 2, 80, 256), BF16),
            pltpu.VMEM((2, 2, 80, 256), BF16),
            pltpu.VMEM((640, 128), F32),
            pltpu.VMEM((384, 128), BF16),
            pltpu.VMEM((8, 48, 128), BF16),
            pltpu.VMEM((8, 32, 128), F32),
            pltpu.VMEM((8, 48, 128), BF16),
            pltpu.VMEM((8, 32, 128), F32),
            pltpu.VMEM((8, 32, 128), F32),
            pltpu.VMEM((8, 48, 128), BF16),
            dma((6,)),
            dma((2,)),
            dma((2,)),
            dma((4,)),
            dma((4,)),
            dma((8, 8)),
            dma((8, 8)),
        ],
        compiler_params=pltpu.CompilerParams(collective_id=0, has_side_effects=True, vmem_limit_bytes=40 << 20),
    )(*(pltpu.with_memory_space_constraint(a, pltpu.HBM) for a in (latents, conv_weight, norm_gain, depth_target)))
    count = 960 * lax.axis_size("tm") * lax.axis_size("row")
    return pl.pallas_call(
        functools.partial(write_kernel, 1.0 / count),
        out_shape=(
            jax.ShapeDtypeStruct((2, 6, 80, 256), BF16),
            jax.ShapeDtypeStruct((256, 256), F32),
            jax.ShapeDtypeStruct((256, 128), F32),
        ),
        in_specs=[vmem, vmem],
        out_specs=(anywhere, anywhere, anywhere),
        scratch_shapes=[pltpu.VMEM((256, 256), F32), pltpu.VMEM((256, 128), F32), dma((3,))],
        compiler_params=pltpu.CompilerParams(vmem_limit_bytes=40 << 20),
    )(feat, fin)


def solution(mesh):
    in_specs = (P("tm", "row", None, None), P(), P(), P("tm", "row", None, None))
    out_specs = (P("tm", "row", None, None), P(), P())
    return jax.shard_map(
        on_device, mesh=mesh, in_specs=in_specs, out_specs=out_specs, check_vma=False
    )
```
